32 devices in a mesh: wide: 8 (over z, y), narrow: 4 (over x, core).
Axes of the slice: x: 2, y: 2, z: 4, core: 2. Of those that a mesh axis runs over, the one named last changes fastest.
Arguments:
- residual: bfloat16 [8, 4, 2048, 256], P('wide', 'narrow'), may hold values from -6 to 6
- scaling: float32 [8, 4, 2048], P('wide', 'narrow'), may hold values from 0.25 to 1
- local_inverse: bfloat16 [8, 4, 2048, 2048], P('wide', 'narrow'), may hold values from -0.125 to 0.125
- coarse_basis: bfloat16 [8, 4, 24, 2048], P('wide', 'narrow'), may hold values from -0.125 to 0.125
- primal_map: int32 [8, 4, 24], P('wide', 'narrow'), may hold values from 0 to 95
- slot_index: int32 [8, 4, 6, 256], P('wide', 'narrow'), may hold values from 0 to 2047, as said below
- slot_length: int32 [8, 4, 6], P('wide', 'narrow'), may hold values from 0 to 256, as said below
- coarse_sub: float32 [8, 96, 96], P('wide'), may hold values from -0.625 to 0.625
- coarse_pivot: float32 [8, 96, 96], P('wide'), as said below
Outputs:
- interface_sum: float32 [8, 4, 2048, 256], P('wide', 'narrow')
The draws below stay inside these ranges and needn't reach their ends.
Inputs may be any that keep to these rules, and one draw needn't show every extreme that they name: `slot_index`: within one slot of one subdomain the 256 entries are distinct. `slot_length`: paired slots have equal lengths: slot j of subdomain (w, n) and slot n of (w, j); slot 4 of (w, n) and slot 5 of (w - 1, n). A subdomain's own narrow slot n, the slot 4 of slab 0 and the slot 5 of slab 8 - 1 have length 0. `coarse_pivot`: Symmetric.
All inputs are finite; a program needn't handle non-finite values.
Results may differ from the reference program's by a relative error of at most 0.0039.
The reference program's roundings to bfloat16 on the way (of `weighted`, `combined`, `outgoing` and `incoming`) count: a program that leaves them out, or rounds other values in their place, can miss the bound.
Values may be sent and summed in bfloat16 or wider, within the bound.
No kernel may reach another device: no remote copies, remote signals or barrier semaphores. Data moves between devices by JAX's collectives and lax.ppermute only.
A program may use at most 128 MiB of HBM per device.

```python
import math
import jax
import jax.numpy as jnp
from jax import lax

NI = 2048
R = 256
P_SIZE = 24
B = 256
NW = 8
NN = 4
G = 96


def draw_slot_length(key, part):
    first_key, second_key = jax.random.split(jax.random.fold_in(key, 11))
    paired = jax.random.randint(first_key, (NW, NN, NN), B // 4, B + 1)
    paired = paired.at[:, 0, 1].set(B)
    counter = jnp.arange(NN)
    upper_tri = counter[:, None] < counter[None, :]
    narrow = jnp.where(upper_tri[None], paired, jnp.swapaxes(paired, 1, 2))
    narrow = jnp.where((counter[:, None] == counter[None, :])[None], 0, narrow)
    links = jax.random.randint(second_key, (NW, NN), B // 4, B + 1)
    slabs = jnp.arange(NW)[:, None]
    upper = jnp.where(slabs < NW - 1, links, 0)
    lower = jnp.where(slabs > 0, jnp.roll(links, 1, axis=0), 0)
    return jnp.concatenate([narrow, lower[:, :, None], upper[:, :, None]], axis=2).astype(jnp.int32)


def draw_slot_index(key, part):
    scores = jax.random.randint(jax.random.fold_in(key, 23), (NW, NN, NN + 2, NI), 0, 1024)
    scores = scores * NI + jnp.arange(NI, dtype=jnp.int32)
    scores = scores.at[0, 0, 0, 0].set(-2)
    scores = scores.at[0, 0, 0, NI - 1].set(-1)
    order = jnp.argsort(scores, axis=-1)
    return order[..., :B].astype(jnp.int32)


def draw_coarse_pivot(key, part):
    first_key, second_key = jax.random.split(jax.random.fold_in(key, 37))
    offdiag = jax.random.uniform(first_key, (NW, G, G), jnp.float32, -1.0, 1.0) * (2.0 / G)
    offdiag = 0.5 * (offdiag + jnp.swapaxes(offdiag, 1, 2))
    diagonal = jax.random.uniform(second_key, (NW, G), jnp.float32, 0.5, 2.0)
    identity = jnp.eye(G, dtype=jnp.float32)
    return (offdiag * (1.0 - identity)[None] + diagonal[:, :, None] * identity[None]).astype(jnp.float32)


def with_ends(values, own_key, least, largest):
    longest = values.shape.index(max(values.shape))
    spots = []
    for shift in (0, 1):
        where = [jax.random.randint(jax.random.fold_in(own_key, axis), (), 0, length) for axis, length in enumerate(values.shape)]
        where[longest] = (where[longest] + shift) % values.shape[longest]
        spots.append(tuple(where))
    return values.at[spots[0]].set(least).at[spots[1]].set(largest)


def levels(key, dims, shards, low, high):
    loudness, own = 1.0, jax.random.fold_in(key, 6)
    for position, parts in shards:
        steps = jnp.exp(jax.random.uniform(jax.random.fold_in(own, position), (parts,), jnp.float32, low / len(shards), high / len(shards)))
        loudness = loudness * jnp.repeat(steps, dims[position] // parts).reshape([-1 if axis == position else 1 for axis in range(len(dims))])
    return loudness


def centred(own_key, extent, width, reach, shards=(), kind=jnp.bfloat16):
    gain = levels(own_key, extent, shards, -0.22, 0.18) if shards else 1.0
    entries = jax.random.normal(own_key, extent, jnp.float32) * width * gain
    return jnp.minimum(jnp.maximum(entries, -reach), reach).astype(kind)


def setup_inputs(seed: int = 0) -> dict:
    keys = jax.random.split(jax.random.key(seed), 10)
    residual = centred(keys[0], (NW, NN, NI, R), 1.0, 6.0, ((0, 8), (1, 4)))
    scaling = jnp.clip(jnp.exp(math.log(1.0) - 1.3862944 * jax.random.uniform(keys[1], (NW, NN, NI), jnp.float32) ** levels(keys[1], (NW, NN, NI), ((0, 8), (1, 4)), -0.2, 0.2)), 0.25, 1.0)
    local_inverse = centred(keys[2], (NW, NN, NI, NI), NI ** -0.5, 0.125, ((0, 8), (1, 4)))
    coarse_basis = centred(keys[3], (NW, NN, P_SIZE, NI), NI ** -0.5, 0.125, ((0, 8), (1, 4)))
    primal_map = with_ends(jax.random.randint(keys[4], (NW, NN, P_SIZE), 0, G), jax.random.fold_in(keys[4], 1), 0, G - 1).astype(jnp.int32)
    slot_index = draw_slot_index(jax.random.fold_in(keys[9], 71), 0)
    slot_length = draw_slot_length(jax.random.fold_in(keys[9], 71), 0)
    coarse_sub = centred(keys[7], (NW, G, G), G ** -0.5, 0.625, ((0, 8),), jnp.float32)
    coarse_pivot = draw_coarse_pivot(jax.random.fold_in(keys[9], 71), 0)
    return {"residual": residual, "scaling": scaling, "local_inverse": local_inverse, "coarse_basis": coarse_basis, "primal_map": primal_map, "slot_index": slot_index, "slot_length": slot_length, "coarse_sub": coarse_sub, "coarse_pivot": coarse_pivot}


highest = lax.Precision.HIGHEST


def exact_dot(left, right):
    return jnp.dot(left, right, precision=highest, preferred_element_type=jnp.float32)


def solve_local(operands):
    return jnp.dot(operands[0], operands[1], preferred_element_type=jnp.float32)


def add_rows(base, where, values):
    return base.at[where.reshape(-1)].add(values.reshape(-1, values.shape[-1]))


def pick_rows(rows, where):
    return rows[where]


def reference(residual, scaling, local_inverse, coarse_basis, primal_map, slot_index, slot_length, coarse_sub, coarse_pivot):
    weighted = (scaling[..., None] * residual.astype(jnp.float32)).astype(jnp.bfloat16)
    flat_inverse = local_inverse.reshape(NW * NN, NI, NI)
    flat_rhs = weighted.reshape(NW * NN, NI, R)
    local_part = lax.map(solve_local, (flat_inverse, flat_rhs)).reshape(NW, NN, NI, R)
    basis_full = coarse_basis.astype(jnp.float32)
    primal = jnp.einsum("wnpi,wnir->wnpr", basis_full, weighted.astype(jnp.float32), precision=highest)
    one_hot = (primal_map[..., None] == jnp.arange(G, dtype=jnp.int32)).astype(jnp.float32)
    coarse_rhs = jnp.einsum("wnpg,wnpr->wgr", one_hot, primal, precision=highest)

    def forward(carry, inputs):
        value = inputs[1] - exact_dot(inputs[0], carry)
        return value, value

    final_y, chain_y = lax.scan(forward, jnp.zeros((G, R), jnp.float32), (coarse_sub, coarse_rhs))
    pivoted = jnp.einsum("wgh,whr->wgr", coarse_pivot, chain_y, precision=highest)

    def backward(carry, inputs):
        solved = inputs[1] - carry
        transfer = exact_dot(inputs[0].T, inputs[1]) - exact_dot(inputs[0].T, carry)
        return transfer, solved

    final_t, coarse_sol = lax.scan(backward, jnp.zeros((G, R), jnp.float32), (coarse_sub, pivoted), reverse=True)
    coarse_vals = jnp.einsum("wnpg,wgr->wnpr", one_hot, coarse_sol, precision=highest)
    spread = jnp.einsum("wnpi,wnpr->wnir", basis_full, coarse_vals, precision=highest)
    combined = (scaling[..., None] * (local_part + spread)).astype(jnp.bfloat16)
    live = jnp.arange(B, dtype=jnp.int32)[None, None, None, :] < slot_length[..., None]
    picked = jax.vmap(jax.vmap(pick_rows))(combined, slot_index)
    outgoing = jnp.where(live[..., None], picked, jnp.zeros((), jnp.bfloat16))
    narrow_in = jnp.swapaxes(outgoing[:, :, :NN], 1, 2)
    zero_slab = jnp.zeros_like(outgoing[:1, :, NN])
    below = jnp.concatenate([zero_slab, outgoing[:-1, :, NN + 1]], axis=0)
    above = jnp.concatenate([outgoing[1:, :, NN], zero_slab], axis=0)
    incoming = jnp.concatenate([narrow_in, below[:, :, None], above[:, :, None]], axis=2)
    return jax.vmap(jax.vmap(add_rows))(combined.astype(jnp.float32), slot_index, incoming.astype(jnp.float32))
```

```python
import jax
import jax.numpy as jnp
from jax import lax
from jax.sharding import PartitionSpec as P

highest = lax.Precision.HIGHEST
f32 = jnp.float32
bf16 = jnp.bfloat16


def swap(block, axis, mask):
    count = lax.axis_size(axis)
    return lax.ppermute(block, axis, [(i, i ^ mask) for i in range(count)])


def swap_odd(block, axis):
    count = lax.axis_size(axis)
    pairs = [(i, i + 1) for i in range(1, count - 1, 2)]
    return lax.ppermute(block, axis, pairs + [(b, a) for a, b in pairs])


def exact(left, right, dims=None):
    if dims is None:
        return jnp.dot(left, right, precision=highest, preferred_element_type=f32)
    return lax.dot_general(left, right, dims, precision=highest, preferred_element_type=f32)


def gather_pairs(block, axis):
    count = lax.axis_size(axis)
    held, offsets, mask = block[None], [0], count // 2
    while mask:
        held = jnp.concatenate([held, swap(held, axis, mask)], axis=0)
        offsets += [o ^ mask for o in offsets]
        mask //= 2
    return held, offsets


def one_hot(index, size, dtype):
    return (index[..., None] == jnp.arange(size, dtype=index.dtype)).astype(dtype)


def body(
    residual,
    scaling,
    local_inverse,
    coarse_basis,
    primal_map,
    slot_index,
    slot_length,
    coarse_sub,
    coarse_pivot,
):
    slabs, groups = lax.axis_size("wide"), lax.axis_size("narrow")
    w, n = lax.axis_index("wide"), lax.axis_index("narrow")
    order = coarse_sub.shape[1]
    basis = coarse_basis[0, 0]
    constraints, rows = basis.shape
    columns = residual.shape[3]
    own_columns = columns // groups
    weights = scaling[0, 0]
    own_map = primal_map[0, 0]

    factors, offsets = gather_pairs(jnp.stack([coarse_sub[0], coarse_pivot[0]]), "wide")
    place = jnp.zeros((slabs,), jnp.int32).at[jnp.array(offsets, jnp.int32) ^ w].set(
        jnp.arange(slabs, dtype=jnp.int32)
    )

    weighted = (weights[:, None] * residual[0, 0].astype(f32)).astype(bf16)
    primal = lax.dot_general(weighted, basis, (((0,), (1,)), ((), ())), preferred_element_type=f32)
    quarter, lanes = own_columns // 4, 32
    packed = jnp.pad(primal, ((0, 0), (0, lanes - constraints)))
    packed = packed.reshape(groups, 4, quarter, lanes)
    tail = jnp.zeros((quarter * (lanes - constraints),), f32).at[:constraints].set(own_map.astype(f32))
    tail = jnp.pad(tail.reshape(quarter, lanes - constraints), ((0, 0), (constraints, 0)))
    packed = packed.at[:, 0].add(tail)
    packed = jnp.swapaxes(packed, 1, 2).reshape(groups, quarter, 4 * lanes)
    sent = jnp.broadcast_to(packed[None], (slabs,) + packed.shape).reshape(
        slabs * groups, quarter, 4 * lanes
    )
    got = lax.all_to_all(sent, ("wide", "narrow"), split_axis=0, concat_axis=0, tiled=True)

    local_part = jnp.dot(local_inverse[0, 0], weighted, preferred_element_type=f32)
    scaled = weights[:, None] * local_part
    parity = w & 1
    picks = jnp.concatenate(
        [n ^ jnp.arange(1, groups), jnp.stack([groups + 1 - parity, groups + parity])]
    )
    indices = slot_index[0, 0][picks]
    lengths = slot_length[0, 0][picks]
    slots, capacity = indices.shape
    live = jnp.arange(capacity, dtype=jnp.int32)[None, :] < lengths[:, None]
    targets = jnp.where(live, indices, -1).reshape(-1)
    chosen = scaled.astype(bf16)[indices]
    scaled_basis = weights[None, :] * basis.astype(f32)
    basis_high = scaled_basis.astype(bf16)
    basis_low = (scaled_basis - basis_high.astype(f32)).astype(bf16)
    basis_both = jnp.concatenate([basis_high, basis_low], axis=0)
    picked_basis = jnp.swapaxes(basis_both[:, indices], 0, 1)
    outgoing = jnp.concatenate([chosen, picked_basis], axis=1)
    arrived = [swap(outgoing[k - 1], "narrow", k) for k in range(1, groups)]
    arrived += [swap(outgoing[groups - 1], "wide", 1), swap_odd(outgoing[groups], "wide")]
    arrived = jnp.stack(arrived)
    scatter = (jnp.arange(rows, dtype=jnp.int32)[:, None] == targets[None, :]).astype(bf16)
    early = jnp.dot(
        scatter, arrived[:, :capacity].reshape(-1, columns), preferred_element_type=f32
    )
    late_basis = jnp.einsum(
        "ikb,kpb->kip",
        scatter.reshape(rows, slots, capacity),
        arrived[:, capacity:],
        preferred_element_type=f32,
    )
    late_basis = late_basis[..., :constraints] + late_basis[..., constraints:]

    got = got.reshape(slabs, groups, quarter, 4, lanes)
    maps = got[:, :, :, 0, constraints:].reshape(slabs, groups, -1)[..., :constraints]
    maps = maps.astype(jnp.int32)
    hots = one_hot(maps, order, f32)
    values = jnp.swapaxes(got[..., :constraints], 2, 3).reshape(
        slabs, groups, own_columns, constraints
    )
    right = jnp.einsum("vmcp,vmpg->vcg", values, hots, precision=highest)

    subs = factors[:, 0][place]
    pivots = factors[:, 1][place]
    flip = (((1,), (1,)), ((), ()))
    chain, carry = [], None
    for v in range(slabs):
        carry = right[v] if v == 0 else right[v] - exact(carry, subs[v], flip)
        chain.append(carry)
    pivoted = [exact(chain[v], pivots[v]) for v in range(slabs)]
    solved, carry = [None] * slabs, None
    for v in reversed(range(slabs)):
        solved[v] = pivoted[v] if carry is None else pivoted[v] - carry
        if v:
            carry = exact(solved[v], subs[v])
    solved = jnp.stack(solved)
    above = jnp.clip(jnp.stack([w ^ 1, w - 1 + 2 * parity]), 0, slabs - 1)
    mine = jnp.broadcast_to(solved[w][None], (groups, own_columns, order))
    sides = [
        jnp.einsum("cg,mpg->mcp", solved[above[i]], hots[above[i]], precision=highest)
        for i in range(2)
    ]
    share = jnp.concatenate([mine] + sides, axis=2)
    share = share[n ^ jnp.arange(groups)]
    pieces = [share[0]] + [swap(share[k], "narrow", k) for k in range(1, groups)]
    solution_t = jnp.stack(pieces)[n ^ jnp.arange(groups)].reshape(columns, -1)

    slab_t, first_t, second_t = (
        solution_t[:, :order],
        solution_t[:, order : order + constraints],
        solution_t[:, order + constraints :],
    )
    near = hots[w]
    joined = sum(exact(late_basis[k - 1], near[n ^ k]) for k in range(1, groups))
    late = exact(
        jnp.concatenate([joined, late_basis[groups - 1], late_basis[groups]], axis=1),
        solution_t,
        flip,
    )
    coarse_vals = exact(one_hot(own_map, order, f32), slab_t, flip)
    spread = exact(basis.astype(f32), coarse_vals, (((0,), (0,)), ((), ())))
    combined = (weights[:, None] * (local_part + spread)).astype(bf16)
    return (combined.astype(f32) + early + late)[None, None]


def solution(mesh):
    in_specs = (
        P("wide", "narrow", None, None),
        P("wide", "narrow", None),
        P("wide", "narrow", None, None),
        P("wide", "narrow", None, None),
        P("wide", "narrow", None),
        P("wide", "narrow", None, None),
        P("wide", "narrow", None),
        P("wide", None, None),
        P("wide", None, None),
    )
    out_specs = P("wide", "narrow", None, None)
    return jax.shard_map(body, mesh=mesh, in_specs=in_specs, out_specs=out_specs, check_vma=False)
```

```python
import functools

import jax
import jax.numpy as jnp
from jax import lax
from jax.experimental import pallas as pl
from jax.experimental.pallas import tpu as pltpu
from jax.sharding import PartitionSpec as P


f32 = jnp.float32
bf16 = jnp.bfloat16
LANES = 128
GROUP = 32


def swap(block, axis, mask):
    count = lax.axis_size(axis)
    return lax.ppermute(block, axis, [(i, i ^ mask) for i in range(count)])


def swap_odd(block, axis):
    count = lax.axis_size(axis)
    pairs = [(i, i + 1) for i in range(1, count - 1, 2)]
    return lax.ppermute(block, axis, pairs + [(b, a) for a, b in pairs])


def ceil_lanes(size):
    return -(-size // LANES) * LANES


def iota(shape, axis):
    return lax.broadcasted_iota(jnp.int32, shape, axis)


def dot(left, right):
    return jnp.dot(left, right, preferred_element_type=f32)


def split_two(value):
    high = value.astype(bf16)
    return high, (value - high.astype(f32)).astype(bf16)


def split_three(value):
    high = value.astype(bf16)
    rest = value - high.astype(f32)
    middle = rest.astype(bf16)
    return high, middle, (rest - middle.astype(f32)).astype(bf16)


def turned_scale(scale_ref):
    scale = scale_ref[...]
    return jnp.concatenate(
        [scale, jnp.zeros((LANES - scale.shape[0], LANES), f32)], axis=0
    ).T


def fixed(shape):
    return pl.BlockSpec(shape, lambda i: (0,) * len(shape))


def call(kernel, outs, in_specs, args, grid=(1,), out_specs=None, scratch=(), flops=0, limit=24):
    many = isinstance(outs, (list, tuple))
    if out_specs is None:
        out_specs = [fixed(o.shape) for o in outs] if many else fixed(outs.shape)
    in_specs = [fixed(a.shape) if s is None else s for s, a in zip(in_specs, args)]
    sizes = [a.size * a.dtype.itemsize for a in list(args) + (list(outs) if many else [outs])]
    return pl.pallas_call(
        kernel,
        out_shape=outs,
        grid=grid,
        in_specs=in_specs,
        out_specs=out_specs,
        scratch_shapes=list(scratch),
        compiler_params=pltpu.CompilerParams(vmem_limit_bytes=limit << 20),
        cost_estimate=pl.CostEstimate(flops=flops, bytes_accessed=sum(sizes), transcendentals=0),
    )(*args)


def join_kernel(*refs):
    start = 0
    for ref in refs[:-2]:
        refs[-1][start : start + ref.shape[0]] = ref[...]
        start += ref.shape[0]


def join(parts, after):
    total = sum(p.shape[0] for p in parts)
    out = jax.ShapeDtypeStruct((total,) + parts[0].shape[1:], parts[0].dtype)
    corner = pl.BlockSpec((16, LANES), lambda i: (0, 0))
    return call(join_kernel, out, [None] * len(parts) + [corner], (*parts, after))


def copies(sources, targets, sems):
    moves = [pltpu.make_async_copy(a, b, sems.at[i]) for i, (a, b) in enumerate(zip(sources, targets))]
    for move in moves:
        move.start()
    return moves


def front_kernel(slabs, groups, res_any, scale_any, basis_any, map_any, weighted_any, sent_ref, res_ref, scale_ref, basis_ref, map_ref, weighted_ref, in_sems, out_sems):
    rows = res_ref.shape[0]
    chunk = min(rows, 512)
    parts = [pl.ds(i * chunk, chunk) for i in range(rows // chunk)]
    sources = [scale_any, basis_any, map_any] + [res_any.at[p] for p in parts]
    targets = [scale_ref, basis_ref, map_ref] + [res_ref.at[p] for p in parts]
    moves = copies(sources, targets, in_sems)
    for move in moves[:3]:
        move.wait()
    scale_turned = turned_scale(scale_ref)
    primal, leaving = None, []
    for i, p in enumerate(parts):
        moves[3 + i].wait()
        for j in range(chunk // LANES):
            here = slice(i * chunk + j * LANES, i * chunk + (j + 1) * LANES)
            column = i * (chunk // LANES) + j
            factor = scale_turned[:, column : column + 1]
            weighted_ref[here, :] = (factor * res_ref[here, :].astype(f32)).astype(bf16)
        leave = pltpu.make_async_copy(weighted_ref.at[p], weighted_any.at[p], out_sems.at[i])
        leave.start()
        leaving.append(leave)
        term = dot(basis_ref[:, i * chunk : (i + 1) * chunk], weighted_ref[i * chunk : (i + 1) * chunk, :])
        primal = term if primal is None else primal + term
    constraints, columns = primal.shape
    turned = jnp.concatenate([primal, jnp.zeros((LANES - constraints, columns), f32)], axis=0).T
    quarter = sent_ref.shape[1]
    spare = GROUP - constraints
    code = map_ref[...].astype(f32)
    code = jnp.concatenate([code, jnp.zeros((1, LANES - constraints), f32)], axis=1)
    lanes = iota((1, LANES), 1)
    tail = jnp.zeros((1, LANES), f32)
    for q in range(-(-constraints // spare)):
        start = GROUP * q + constraints
        inside = (lanes >= start) & (lanes < start + min(spare, constraints - spare * q))
        tail = jnp.where(inside, pltpu.roll(code, start - spare * q, 1), tail)
    tail = jnp.where(iota((quarter, LANES), 0) == 0, tail, 0.0)
    for m in range(groups):
        piece = tail
        for g in range(4):
            start = (m * 4 + g) * quarter
            part = turned[start : start + quarter, :]
            piece = piece + (pltpu.roll(part, GROUP * g, 1) if g else part)
        for v in range(slabs):
            sent_ref[v * groups + m] = piece
    for leave in leaving:
        leave.wait()


def scale_columns(turned_ref, step, block):
    lanes = iota((LANES, LANES), 1)
    for j in range(block // LANES):
        hit = jnp.where(lanes == step * (block // LANES) + j, turned_ref[...], 0.0)
        yield jnp.sum(hit, axis=1, keepdims=True)


def place_of():
    return lax.axis_index("wide"), lax.axis_index("narrow")


def slot_rows(groups):
    w, n = place_of()
    parity = w & 1
    return [n ^ k for k in range(1, groups)] + [groups + 1 - parity, groups + parity]


def local_kernel(inverse_any, weighted_any, scale_any, part_ref, narrow_ref, mark_ref, inverse_ref, weighted_ref, scale_ref, turned_ref, sems):
    rows = inverse_ref.shape[0]
    block = min(rows, 256)
    steps = rows // block
    sources, targets = [scale_any, weighted_any], [scale_ref, weighted_ref]
    for i in range(steps):
        p = pl.ds(i * block, block)
        sources.append(inverse_any.at[p])
        targets.append(inverse_ref.at[p])
    moves = copies(sources, targets, sems)
    for move in moves[:2]:
        move.wait()
    turned_ref[...] = turned_scale(scale_ref)
    mark_ref[...] = jnp.zeros_like(mark_ref)

    def one(i, carry):
        p = pl.ds(pl.multiple_of(i * block, block), block)
        pltpu.make_async_copy(inverse_any.at[p], inverse_ref.at[p], sems.at[2 + i]).wait()
        part = dot(inverse_ref[p, :], weighted_ref[...])
        factors = scale_columns(turned_ref, i, block)
        scaled = jnp.concatenate(list(factors), axis=0) * part
        part_ref[p, :] = scaled
        narrow_ref[p, :] = scaled.astype(bf16)
        return carry

    lax.fori_loop(0, steps, one, 0)


def pick_kernel(groups, narrow_ref, lane_scale_ref, basis_ref, index_ref, *rest):
    slots = groups + 1
    outs, basis = rest[:slots], rest[slots]
    capacity = index_ref.shape[2]
    constraints, total = basis_ref.shape
    picks = [index_ref[r] for r in slot_rows(groups)]
    rows = picks + [jnp.zeros((LANES - slots, capacity), jnp.int32)]
    columns_of = jnp.concatenate(rows, axis=0).astype(f32).T
    basis[...] = lane_scale_ref[...] * basis_ref[...].astype(f32)
    lanes = iota((capacity, LANES), 1).astype(f32)
    for k in range(slots):
        spot = jnp.broadcast_to(columns_of[:, k : k + 1], (capacity, LANES))
        hots = [(spot == lanes + float(j * LANES)).astype(f32).astype(bf16) for j in range(total // LANES)]
        outs[k][:capacity, :] = dot(jnp.concatenate(hots, axis=1), narrow_ref[...]).astype(bf16)
        parts = []
        for c in range(capacity // LANES):
            spot = jnp.broadcast_to(picks[k][:, c * LANES : (c + 1) * LANES], (constraints, LANES))
            inner, outer = spot & (LANES - 1), spot // LANES
            value = jnp.zeros((constraints, LANES), f32)
            for j in range(total // LANES):
                found = jnp.take_along_axis(basis[:, j * LANES : (j + 1) * LANES], inner, axis=1)
                value = jnp.where(outer == j, found, value)
            parts.append(value)
        fill = jnp.zeros((GROUP - constraints, capacity), f32)
        outs[k][capacity:, :] = jnp.concatenate([jnp.concatenate(parts, axis=1), fill], axis=0).astype(bf16)


def unpack_kernel(slabs, groups, constraints, got_ref, right_ref, maps_ref):
    pieces, quarter, _ = got_ref.shape
    spare = GROUP - constraints
    heads = jnp.concatenate([got_ref[i, 0:1, :] for i in range(pieces)], axis=0)
    lanes = iota((pieces, LANES), 1)
    maps = jnp.full((pieces, LANES), -1.0, f32)
    for q in range(-(-constraints // spare)):
        shift = (spare * q - GROUP * q - constraints) % LANES
        moved = pltpu.roll(heads, shift, 1) if shift else heads
        inside = (lanes >= spare * q) & (lanes < min(spare * (q + 1), constraints))
        maps = jnp.where(inside, moved, maps)
    maps_ref[...] = maps
    order = right_ref.shape[2]
    halves = groups * GROUP // LANES
    lanes = iota((quarter, LANES), 1) // GROUP
    wide = iota((1, LANES), 1) // GROUP

    def one(v, carry):
        value, codes = [], []
        for h in range(halves):
            rows = []
            for g in range(4):
                row = None
                for j in range(4):
                    part = got_ref[v * groups + 4 * h + j]
                    shift = (GROUP * (j - g)) % LANES
                    part = pltpu.roll(part, shift, 1) if shift else part
                    row = part if row is None else jnp.where(lanes == j, part, row)
                rows.append(row)
            value.append(jnp.concatenate(rows, axis=0))
            code = None
            for j in range(4):
                part = maps_ref[pl.ds(v * groups + 4 * h + j, 1), :]
                part = pltpu.roll(part, GROUP * j, 1) if j else part
                code = part if code is None else jnp.where(wide == j, part, code)
            codes.append(code)
        value = jnp.concatenate(value, axis=1) if halves > 1 else value[0]
        code = jnp.concatenate(codes, axis=1) if halves > 1 else codes[0]
        hot = (iota((order, halves * LANES), 0).astype(f32) == code).astype(f32).astype(bf16)
        stacked = jnp.concatenate(split_three(value), axis=0)
        total = lax.dot_general(stacked, hot, (((1,), (1,)), ((), ())), preferred_element_type=f32)
        c = value.shape[0]
        right_ref[v] = total[:c] + total[c : 2 * c] + total[2 * c :]
        return carry

    lax.fori_loop(0, slabs, one, 0, unroll=slabs <= 8)


def solve_kernel(slabs, groups, constraints, offsets, right_ref, maps_ref, *rest):
    count = len(offsets).bit_length()
    mine, other = rest[:count], rest[count : 2 * count]
    shares = rest[2 * count : 2 * count + groups]
    raw, forward, backward, pivots, solved = rest[2 * count + groups :]
    w, n = place_of()
    core = n & 1
    size = mine[0].shape[1]
    order = raw.shape[2]
    if size != order:
        raw[...] = jnp.zeros_like(raw)
    start = 0
    for a, b in zip(mine, other):
        for i in range(a.shape[0]):
            slab = w ^ offsets[start + i]
            raw[core, slab, :size, :size] = a[i]
            raw[1 - core, slab, :size, :size] = b[i]
        start += a.shape[0]
    c = right_ref.shape[1]
    few = slabs <= 8

    def prepare(v, carry):
        sub = raw[0, v]
        for ref, value in ((forward, sub.T), (backward, sub), (pivots, raw[1, v])):
            high, low = split_two(value)
            ref[v, :, :order] = high
            ref[v, :, order:] = low
        return carry

    def times(value, factor):
        total = dot(jnp.concatenate(split_two(value), axis=0), factor)
        return total[:c, :order] + (total[:c, order:] + total[c:, :order])

    def down(v, value):
        value = right_ref[v] - times(value, forward[v])
        solved[v] = value
        return value

    def pivot(v, carry):
        solved[v] = times(solved[v], pivots[v])
        return carry

    def up(i, value):
        v = slabs - 2 - i
        value = solved[v] - times(value, backward[v + 1])
        solved[v] = value
        return value

    lax.fori_loop(0, slabs, prepare, 0, unroll=few)
    solved[0] = right_ref[0]
    lax.fori_loop(1, slabs, down, right_ref[0], unroll=few)
    lax.fori_loop(0, slabs, pivot, 0, unroll=few)
    lax.fori_loop(0, slabs - 1, up, solved[slabs - 1], unroll=few)

    parity = w & 1
    sides = [w, w ^ 1, jnp.clip(w - 1 + 2 * parity, 0, slabs - 1)]
    value = jnp.concatenate([solved[s] for s in sides], axis=1)
    stacked = jnp.concatenate(split_three(value), axis=0)
    width = shares[0].shape[1]
    lanes = iota((1, width), 1)
    rows = iota((order, width), 0).astype(f32)
    starts = [
        [size + (2 + i) * constraints for i in range(3)],
        [size],
        [size + constraints],
    ]
    for k in range(groups):
        hots = []
        for s, (side, places) in enumerate(zip(sides, starts)):
            code = maps_ref[pl.ds(side * groups + (n ^ k), 1), :]
            code = jnp.concatenate([code, jnp.full((1, width - LANES), -1.0, f32)], axis=1)
            full = jnp.where(lanes < size, lanes.astype(f32), -1.0) if s == 0 else jnp.full((1, width), -1.0, f32)
            for place in places:
                inside = (lanes >= place) & (lanes < place + constraints)
                full = jnp.where(inside, pltpu.roll(code, place, 1), full)
            hots.append((rows == full).astype(f32).astype(bf16))
        total = dot(stacked, jnp.concatenate(hots, axis=0))
        shares[k][...] = total[:c] + total[c : 2 * c] + total[2 * c :]


def scatter_kernel(groups, size, length_ref, index_ref, maps_ref, lane_scale_ref, basis_ref, *rest):
    slots = groups + 1
    arrived = rest[:slots]
    early_ref, late_ref, own_ref, joined, targets = rest[slots:]
    step = pl.program_id(0)
    columns, width = early_ref.shape[1], late_ref.shape[1]
    block = early_ref.shape[0] // pl.num_programs(0)
    here_rows = pl.ds(pl.multiple_of(step * block, block), block)
    constraints = basis_ref.shape[0]
    capacity = index_ref.shape[2]
    w, n = place_of()

    @pl.when(step == 0)
    def _():
        for k, r in enumerate(slot_rows(groups)):
            spot = index_ref[r]
            live = iota((1, capacity), 1) < length_ref[r]
            targets[:, k * capacity : (k + 1) * capacity] = jnp.where(live, spot, -1)
            here = slice(k * capacity, (k + 1) * capacity)
            joined[here, :columns] = arrived[k][:capacity, :]
            lanes = iota((1, LANES), 1)
            if k < groups - 1:
                code = maps_ref[pl.ds(w * groups + (n ^ (k + 1)), 1), :]
            else:
                start = size + (k - groups + 1) * constraints
                code = jnp.where(lanes < constraints, lanes + start, -1).astype(f32)
            hot = (iota((width, LANES), 0).astype(f32) == code).astype(f32).astype(bf16)
            spread = dot(hot[:, :GROUP], arrived[k][capacity:, :])
            joined[here, columns:] = spread.T.astype(bf16)

    rows = iota((block, capacity), 0) + step * block
    hots = []
    for k in range(slots):
        target = targets[:, k * capacity : (k + 1) * capacity]
        hots.append((rows == target).astype(f32).astype(bf16))
    total = dot(jnp.concatenate(hots, axis=1), joined[...])
    early_ref[here_rows, :] = total[:, :columns]
    late_ref[here_rows, :] = total[:, columns:].astype(bf16)
    scaled = lane_scale_ref[...] * basis_ref[...].astype(f32)
    high = scaled.astype(bf16).astype(f32)
    start = size + 2 * constraints
    stop = start + 3 * constraints
    stack = jnp.concatenate(
        [jnp.zeros((start, block), f32), high, scaled - high, high, jnp.zeros((width - stop, block), f32)],
        axis=0,
    )
    own_ref[here_rows, :] = stack.T.astype(bf16)


def final_kernel(groups, size, constraints, part_ref, early_ref, late_ref, own_ref, *rest):
    pieces = rest[:groups]
    out_ref, values, highs, lows, owns = rest[groups:]
    _, n = place_of()

    @pl.when(pl.program_id(0) == 0)
    def _():
        c = pieces[0].shape[0]
        for k in range(groups):
            values[pl.ds(pl.multiple_of((n ^ k) * c, c), c), :] = pieces[k][...]
        value = values[...].T
        high = value.astype(bf16).astype(f32)
        low = value - high
        highs[...] = high.astype(bf16)
        lows[...] = low.astype(bf16)
        upper = iota(value.shape, 0) < size + 4 * constraints
        owns[...] = jnp.where(upper, high, low).astype(bf16)

    block = out_ref.shape[0]
    here = pl.ds(pl.multiple_of(pl.program_id(0) * block, block), block)
    late = late_ref[here, :]
    combined = (part_ref[here, :] + dot(own_ref[here, :], owns[...])).astype(bf16).astype(f32)
    out_ref[...] = combined + (early_ref[here, :] + (dot(late, highs[...]) + dot(late, lows[...])))


def body(
    residual,
    scaling,
    local_inverse,
    coarse_basis,
    primal_map,
    slot_index,
    slot_length,
    coarse_sub,
    coarse_pivot,
):
    slabs, groups = lax.axis_size("wide"), lax.axis_size("narrow")
    n = lax.axis_index("narrow")
    residual, inverse = residual[0, 0], local_inverse[0, 0]
    basis = coarse_basis[0, 0]
    slots, capacity = slot_index.shape[2] - 1, slot_index.shape[3]
    index = slot_index.reshape(slots + 1, 1, capacity)
    length = slot_length[0, 0]
    size = coarse_sub.shape[1]
    order = ceil_lanes(size)
    rows, columns = residual.shape
    constraints = basis.shape[0]
    own_columns = columns // groups
    quarter = own_columns // 4
    width = ceil_lanes(size + 5 * constraints)
    scale = scaling[0, 0].reshape(rows // LANES, LANES)
    lane_scale = scaling[0]
    smem = pl.BlockSpec(memory_space=pltpu.SMEM)
    struct = jax.ShapeDtypeStruct

    def by_rows(block, cols):
        return pl.BlockSpec((block, cols), lambda i: (i, 0))

    def by_lanes(count, block):
        return pl.BlockSpec((count, block), lambda i: (0, i))

    any_space = pl.BlockSpec(memory_space=pl.ANY)
    vmem = pl.BlockSpec(memory_space=pltpu.VMEM)
    factor = jnp.where((n & 1) == 0, coarse_sub, coarse_pivot)
    chunks = -(-rows // 512)
    weighted, sent = call(
        functools.partial(front_kernel, slabs, groups),
        [struct((rows, columns), bf16), struct((slabs * groups, quarter, LANES), f32)],
        [any_space] * 4,
        (residual, scale, basis, primal_map[0]),
        out_specs=[any_space, fixed((slabs * groups, quarter, LANES))],
        scratch=[
            pltpu.VMEM((rows, columns), bf16),
            pltpu.VMEM(scale.shape, f32),
            pltpu.VMEM(basis.shape, bf16),
            pltpu.VMEM(primal_map[0].shape, jnp.int32),
            pltpu.VMEM((rows, columns), bf16),
            pltpu.SemaphoreType.DMA((3 + chunks,)),
            pltpu.SemaphoreType.DMA((chunks,)),
        ],
        flops=2 * constraints * rows * columns,
        limit=62,
    )
    got = lax.all_to_all(sent, ("wide", "narrow"), split_axis=0, concat_axis=0, tiled=True)

    part, narrow, mark = call(
        local_kernel,
        [struct((rows, columns), f32), struct((rows, columns), bf16), struct((16, LANES), f32)],
        [any_space] * 3,
        (inverse, weighted, scale),
        out_specs=[vmem] * 3,
        scratch=[
            pltpu.VMEM((rows, rows), bf16),
            pltpu.VMEM((rows, columns), bf16),
            pltpu.VMEM(scale.shape, f32),
            pltpu.VMEM((LANES, LANES), f32),
            pltpu.SemaphoreType.DMA((2 + rows // min(rows, 256),)),
        ],
        flops=2 * rows * columns * rows,
        limit=57,
    )
    outgoing = call(
        functools.partial(pick_kernel, groups),
        [struct((capacity + GROUP, columns), bf16)] * slots,
        [vmem] + [None] * 3,
        (narrow, lane_scale, basis, index),
        scratch=[pltpu.VMEM((constraints, rows), f32)],
        flops=2 * rows * columns * slots * capacity,
    )
    waits = [weighted] + [mark] * slabs
    mine, held, offsets, mask = [factor], factor, [0], slabs // 2
    while mask:
        mine.append(swap(held, "wide", mask))
        offsets = offsets + [o ^ mask for o in offsets]
        mask //= 2
        if mask:
            held = join(mine, waits[len(mine) - 2])
    other = []
    for piece in mine:
        other.append(swap(piece, "narrow", 1))
    arrived = []
    for k in range(slots):
        if k < groups - 1:
            arrived.append(swap(outgoing[k], "narrow", k + 1))
        elif k == groups - 1:
            arrived.append(swap(outgoing[k], "wide", 1))
        else:
            arrived.append(swap_odd(outgoing[k], "wide"))

    right, maps = call(
        functools.partial(unpack_kernel, slabs, groups, constraints),
        [struct((slabs, own_columns, order), f32), struct((slabs * groups, LANES), f32)],
        [None],
        (got,),
        flops=2 * slabs * 3 * own_columns * LANES * order,
    )
    shares = call(
        functools.partial(solve_kernel, slabs, groups, constraints, offsets),
        [struct((own_columns, width), f32)] * groups,
        [None] * (2 + len(mine) + len(other)),
        (right, maps, *mine, *other),
        scratch=[
            pltpu.VMEM((2, slabs, order, order), f32),
            pltpu.VMEM((slabs, order, 2 * order), bf16),
            pltpu.VMEM((slabs, order, 2 * order), bf16),
            pltpu.VMEM((slabs, order, 2 * order), bf16),
            pltpu.VMEM((slabs, own_columns, order), f32),
        ],
        flops=2 * 3 * slabs * 2 * own_columns * order * 2 * order,
        limit=24 if slabs <= 8 else 62,
    )
    pieces = [shares[0]] + [swap(shares[k], "narrow", k) for k in range(1, groups)]

    block = min(rows, 512)
    early, late, own = call(
        functools.partial(scatter_kernel, groups, size),
        [struct((rows, columns), f32), struct((rows, width), bf16), struct((rows, width), bf16)],
        [smem, None, None, by_lanes(1, block), by_lanes(constraints, block)] + [None] * slots,
        (length, index, maps, lane_scale, basis, *arrived),
        grid=(rows // block,),
        out_specs=[vmem] * 3,
        scratch=[
            pltpu.VMEM((slots * capacity, columns + width), bf16),
            pltpu.VMEM((1, slots * capacity), jnp.int32),
        ],
        flops=2 * rows * slots * capacity * (columns + width),
    )
    result = call(
        functools.partial(final_kernel, groups, size, constraints),
        struct((rows, columns), f32),
        [vmem] * 4 + [None] * groups,
        (part, early, late, own, *pieces),
        grid=(rows // block,),
        out_specs=by_rows(block, columns),
        scratch=[
            pltpu.VMEM((columns, width), f32),
            pltpu.VMEM((width, columns), bf16),
            pltpu.VMEM((width, columns), bf16),
            pltpu.VMEM((width, columns), bf16),
        ],
        flops=2 * rows * columns * 3 * width,
    )
    return result[None, None]


def solution(mesh):
    in_specs = (
        P("wide", "narrow", None, None),
        P("wide", "narrow", None),
        P("wide", "narrow", None, None),
        P("wide", "narrow", None, None),
        P("wide", "narrow", None),
        P("wide", "narrow", None, None),
        P("wide", "narrow", None),
        P("wide", None, None),
        P("wide", None, None),
    )
    out_specs = P("wide", "narrow", None, None)

    return jax.shard_map(body, mesh=mesh, in_specs=in_specs, out_specs=out_specs, check_vma=False)
```

```python
import functools

import jax
import jax.numpy as jnp
from jax import lax
from jax.experimental import pallas as pl
from jax.experimental.pallas import tpu as pltpu
from jax.sharding import PartitionSpec as P


f32 = jnp.float32
bf16 = jnp.bfloat16
LANES = 128
GROUP = 32


def swap(block, axis, mask):
    count = lax.axis_size(axis)
    return lax.ppermute(block, axis, [(i, i ^ mask) for i in range(count)])


def swap_odd(block, axis):
    count = lax.axis_size(axis)
    pairs = [(i, i + 1) for i in range(1, count - 1, 2)]
    return lax.ppermute(block, axis, pairs + [(b, a) for a, b in pairs])


def ceil_lanes(size):
    return -(-size // LANES) * LANES


def iota(shape, axis):
    return lax.broadcasted_iota(jnp.int32, shape, axis)


def dot(left, right):
    return jnp.dot(left, right, preferred_element_type=f32)


def split_two(value):
    high = value.astype(bf16)
    return high, (value - high.astype(f32)).astype(bf16)


def split_three(value):
    high = value.astype(bf16)
    rest = value - high.astype(f32)
    middle = rest.astype(bf16)
    return high, middle, (rest - middle.astype(f32)).astype(bf16)


def turned_scale(scale_ref):
    scale = scale_ref[...]
    return jnp.concatenate(
        [scale, jnp.zeros((LANES - scale.shape[0], LANES), f32)], axis=0
    ).T


def fixed(shape):
    return pl.BlockSpec(shape, lambda i: (0,) * len(shape))


def call(kernel, outs, in_specs, args, grid=(1,), out_specs=None, scratch=(), flops=0, limit=24):
    many = isinstance(outs, (list, tuple))
    resident = pl.BlockSpec(memory_space=pltpu.VMEM)
    if out_specs is None:
        out_specs = [resident] * len(outs) if many else resident
    in_specs = [resident if s is None else s for s in in_specs]
    sizes = [a.size * a.dtype.itemsize for a in list(args) + (list(outs) if many else [outs])]
    return pl.pallas_call(
        kernel,
        out_shape=outs,
        grid=grid,
        in_specs=in_specs,
        out_specs=out_specs,
        scratch_shapes=list(scratch),
        compiler_params=pltpu.CompilerParams(vmem_limit_bytes=limit << 20),
        cost_estimate=pl.CostEstimate(flops=flops, bytes_accessed=sum(sizes), transcendentals=0),
    )(*args)


def join_kernel(*refs):
    start = 0
    for ref in refs[:-1]:
        refs[-1][start : start + ref.shape[0]] = ref[...]
        start += ref.shape[0]


def join(parts):
    total = sum(p.shape[0] for p in parts)
    out = jax.ShapeDtypeStruct((total,) + parts[0].shape[1:], parts[0].dtype)
    return call(join_kernel, out, [None] * len(parts), parts)


def copies(sources, targets, sems):
    moves = [pltpu.make_async_copy(a, b, sems.at[i]) for i, (a, b) in enumerate(zip(sources, targets))]
    for move in moves:
        move.start()
    return moves


def weigh(scale_turned, res_ref, start, count):
    for j in range(count // LANES):
        row = start + j * LANES
        factor = scale_turned[:, row // LANES : row // LANES + 1]
        yield (factor * res_ref[row : row + LANES, :].astype(f32)).astype(bf16)


def front_kernel(slabs, groups, res_any, scale_any, basis_any, map_any, sent_ref, res_ref, scale_ref, basis_ref, map_ref, sems):
    rows = res_ref.shape[0]
    chunk = rows // 2
    parts = [pl.ds(i * chunk, chunk) for i in range(rows // chunk)]
    sources = [scale_any, basis_any, map_any] + [res_any.at[p] for p in parts]
    targets = [scale_ref, basis_ref, map_ref] + [res_ref.at[p] for p in parts]
    moves = copies(sources, targets, sems)
    for move in moves[:3]:
        move.wait()
    scale_turned = turned_scale(scale_ref)
    weighted = []
    for i in range(rows // chunk):
        moves[3 + i].wait()
        weighted += list(weigh(scale_turned, res_ref, i * chunk, chunk))
    primal = dot(basis_ref[...], jnp.concatenate(weighted, axis=0))
    constraints, columns = primal.shape
    turned = jnp.concatenate([primal, jnp.zeros((LANES - constraints, columns), f32)], axis=0).T
    quarter = sent_ref.shape[1]
    spare = GROUP - constraints
    code = map_ref[...].astype(f32)
    code = jnp.concatenate([code, jnp.zeros((1, LANES - constraints), f32)], axis=1)
    lanes = iota((1, LANES), 1)
    tail = jnp.zeros((1, LANES), f32)
    for q in range(-(-constraints // spare)):
        start = GROUP * q + constraints
        inside = (lanes >= start) & (lanes < start + min(spare, constraints - spare * q))
        tail = jnp.where(inside, pltpu.roll(code, start - spare * q, 1), tail)
    tail = jnp.where(iota((quarter, LANES), 0) == 0, tail, 0.0)
    for m in range(groups):
        piece = tail
        for g in range(4):
            start = (m * 4 + g) * quarter
            part = turned[start : start + quarter, :]
            piece = piece + (pltpu.roll(part, GROUP * g, 1) if g else part)
        for v in range(slabs):
            sent_ref[v * groups + m] = piece


def place_of():
    return lax.axis_index("wide"), lax.axis_index("narrow")


def slot_rows(groups):
    w, n = place_of()
    parity = w & 1
    return [n ^ k for k in range(1, groups)] + [groups + 1 - parity, groups + parity]


def local_kernel(groups, inverse_any, res_any, scale_any, lane_scale_any, basis_any, index_any, part_any, *rest):
    slots = groups + 1
    outs_any, outs = rest[:slots], rest[slots : 2 * slots]
    lane_scale_ref, basis_ref, index_ref, inverse_ref, res_ref, scale_ref, weighted_ref, narrow_ref, part_ref, scaled_ref, sems, out_sems = rest[2 * slots :]
    rows = inverse_ref.shape[0]
    half = rows // 2
    halves = [pl.ds(i * half, half) for i in range(2)]
    sources = [lane_scale_any, basis_any, index_any, scale_any, res_any]
    targets = [lane_scale_ref, basis_ref, index_ref, scale_ref, res_ref]
    sources += [inverse_any.at[p] for p in halves]
    targets += [inverse_ref.at[p] for p in halves]
    moves = copies(sources, targets, sems)
    for move in moves[:3]:
        move.wait()
    capacity = index_ref.shape[2]
    constraints = basis_ref.shape[0]
    picks = [index_ref[r] for r in slot_rows(groups)]
    scaled_ref[...] = lane_scale_ref[...] * basis_ref[...].astype(f32)
    for k in range(slots):
        parts = []
        for c in range(capacity // LANES):
            spot = jnp.broadcast_to(picks[k][:, c * LANES : (c + 1) * LANES], (constraints, LANES))
            inner, outer = spot & (LANES - 1), spot // LANES
            value = jnp.zeros((constraints, LANES), f32)
            for j in range(rows // LANES):
                found = jnp.take_along_axis(scaled_ref[:, j * LANES : (j + 1) * LANES], inner, axis=1)
                value = jnp.where(outer == j, found, value)
            parts.append(value)
        fill = jnp.zeros((GROUP - constraints, capacity), f32)
        outs[k][capacity:, :] = jnp.concatenate([jnp.concatenate(parts, axis=1), fill], axis=0).astype(bf16)
    for move in moves[3:5]:
        move.wait()
    turned = turned_scale(scale_ref)
    for j, value in enumerate(weigh(turned, res_ref, 0, rows)):
        weighted_ref[j * LANES : (j + 1) * LANES, :] = value
    leaving = []
    for i, p in enumerate(halves):
        moves[5 + i].wait()
        block = min(half, 256)
        for start in range(i * half, (i + 1) * half, block):
            part = dot(inverse_ref[start : start + block, :], weighted_ref[...])
            for j in range(block // LANES):
                row = start + j * LANES
                column = row // LANES
                scaled = turned[:, column : column + 1] * part[j * LANES : (j + 1) * LANES, :]
                part_ref[row : row + LANES, :] = scaled
                narrow_ref[row : row + LANES, :] = scaled.astype(bf16)
        leave = pltpu.make_async_copy(part_ref.at[p], part_any.at[p], out_sems.at[i])
        leave.start()
        leaving.append(leave)
    spare_rows = [jnp.zeros((LANES - slots, capacity), jnp.int32)]
    columns_of = jnp.concatenate(picks + spare_rows, axis=0).astype(f32).T
    lanes = iota((capacity, LANES), 1).astype(f32)
    for k in range(slots):
        spot = jnp.broadcast_to(columns_of[:, k : k + 1], (capacity, LANES))
        hots = [(spot == lanes + float(j * LANES)).astype(f32).astype(bf16) for j in range(rows // LANES)]
        outs[k][:capacity, :] = dot(jnp.concatenate(hots, axis=1), narrow_ref[...]).astype(bf16)
        leave = pltpu.make_async_copy(outs[k], outs_any[k], out_sems.at[2 + k])
        leave.start()
        leaving.append(leave)
    for leave in leaving:
        leave.wait()


def unpack_kernel(slabs, groups, constraints, got_ref, right_ref, maps_ref):
    pieces, quarter, _ = got_ref.shape
    spare = GROUP - constraints
    heads = jnp.concatenate([got_ref[i, 0:1, :] for i in range(pieces)], axis=0)
    lanes = iota((pieces, LANES), 1)
    maps = jnp.full((pieces, LANES), -1.0, f32)
    for q in range(-(-constraints // spare)):
        shift = (spare * q - GROUP * q - constraints) % LANES
        moved = pltpu.roll(heads, shift, 1) if shift else heads
        inside = (lanes >= spare * q) & (lanes < min(spare * (q + 1), constraints))
        maps = jnp.where(inside, moved, maps)
    maps_ref[...] = maps
    order = right_ref.shape[2]
    halves = groups * GROUP // LANES
    lanes = iota((quarter, LANES), 1) // GROUP
    wide = iota((1, LANES), 1) // GROUP

    def one(v, carry):
        value, codes = [], []
        for h in range(halves):
            rows = []
            for g in range(4):
                row = None
                for j in range(4):
                    part = got_ref[v * groups + 4 * h + j]
                    shift = (GROUP * (j - g)) % LANES
                    part = pltpu.roll(part, shift, 1) if shift else part
                    row = part if row is None else jnp.where(lanes == j, part, row)
                rows.append(row)
            value.append(jnp.concatenate(rows, axis=0))
            code = None
            for j in range(4):
                part = maps_ref[pl.ds(v * groups + 4 * h + j, 1), :]
                part = pltpu.roll(part, GROUP * j, 1) if j else part
                code = part if code is None else jnp.where(wide == j, part, code)
            codes.append(code)
        value = jnp.concatenate(value, axis=1) if halves > 1 else value[0]
        code = jnp.concatenate(codes, axis=1) if halves > 1 else codes[0]
        hot = (iota((order, halves * LANES), 0).astype(f32) == code).astype(f32).astype(bf16)
        stacked = jnp.concatenate(split_three(value), axis=0)
        total = lax.dot_general(stacked, hot, (((1,), (1,)), ((), ())), preferred_element_type=f32)
        c = value.shape[0]
        right_ref[v] = total[:c] + total[c : 2 * c] + total[2 * c :]
        return carry

    lax.fori_loop(0, slabs, one, 0, unroll=slabs <= 8)


def solve_kernel(slabs, groups, constraints, offsets, right_ref, maps_ref, *rest):
    count = len(offsets).bit_length()
    held, shares = rest[:count], rest[count : count + groups]
    raw, forward, backward, pivots, solved = rest[count + groups :]
    w, n = place_of()
    size = held[0].shape[2]
    order = raw.shape[2]
    if size != order:
        raw[...] = jnp.zeros_like(raw)
    start = 0
    for ref in held:
        for i in range(ref.shape[0]):
            slab = w ^ offsets[start + i]
            for j in range(2):
                raw[j, slab, :size, :size] = ref[i, j]
        start += ref.shape[0]
    c = right_ref.shape[1]
    few = slabs <= 8

    def prepare(v, carry):
        sub = raw[0, v]
        for ref, value in ((forward, sub.T), (backward, sub), (pivots, raw[1, v])):
            high, low = split_two(value)
            ref[v, :, :order] = high
            ref[v, :, order:] = low
        return carry

    def times(value, factor):
        total = dot(jnp.concatenate(split_two(value), axis=0), factor)
        return total[:c, :order] + (total[:c, order:] + total[c:, :order])

    def down(v, value):
        value = right_ref[v] - times(value, forward[v])
        solved[v] = value
        return value

    def pivot(v, carry):
        solved[v] = times(solved[v], pivots[v])
        return carry

    def up(i, value):
        v = slabs - 2 - i
        value = solved[v] - times(value, backward[v + 1])
        solved[v] = value
        return value

    lax.fori_loop(0, slabs, prepare, 0, unroll=few)
    solved[0] = right_ref[0]
    lax.fori_loop(1, slabs, down, right_ref[0], unroll=few)
    lax.fori_loop(0, slabs, pivot, 0, unroll=few)
    lax.fori_loop(0, slabs - 1, up, solved[slabs - 1], unroll=few)

    parity = w & 1
    sides = [w, w ^ 1, jnp.clip(w - 1 + 2 * parity, 0, slabs - 1)]
    value = jnp.concatenate([solved[s] for s in sides], axis=1)
    stacked = jnp.concatenate(split_three(value), axis=0)
    width = shares[0].shape[1]
    lanes = iota((1, width), 1)
    rows = iota((order, width), 0).astype(f32)
    starts = [
        [size + (2 + i) * constraints for i in range(3)],
        [size],
        [size + constraints],
    ]
    for k in range(groups):
        hots = []
        for s, (side, places) in enumerate(zip(sides, starts)):
            code = maps_ref[pl.ds(side * groups + (n ^ k), 1), :]
            code = jnp.concatenate([code, jnp.full((1, width - LANES), -1.0, f32)], axis=1)
            full = jnp.where(lanes < size, lanes.astype(f32), -1.0) if s == 0 else jnp.full((1, width), -1.0, f32)
            for place in places:
                inside = (lanes >= place) & (lanes < place + constraints)
                full = jnp.where(inside, pltpu.roll(code, place, 1), full)
            hots.append((rows == full).astype(f32).astype(bf16))
        total = dot(stacked, jnp.concatenate(hots, axis=0))
        shares[k][...] = total[:c] + total[c : 2 * c] + total[2 * c :]


def scatter_kernel(groups, size, length_ref, index_ref, maps_ref, lane_scale_ref, basis_ref, *rest):
    slots = groups + 1
    arrived = rest[:slots]
    early_ref, late_ref, own_ref, joined, targets = rest[slots:]
    step = pl.program_id(0)
    columns, width = early_ref.shape[1], late_ref.shape[1]
    block = early_ref.shape[0] // pl.num_programs(0)
    here_rows = pl.ds(pl.multiple_of(step * block, block), block)
    constraints = basis_ref.shape[0]
    capacity = index_ref.shape[2]
    w, n = place_of()

    @pl.when(step == 0)
    def _():
        for k, r in enumerate(slot_rows(groups)):
            spot = index_ref[r]
            count = jnp.where(iota(length_ref.shape, 1) == r, length_ref[...], 0)
            live = iota((1, capacity), 1) < jnp.sum(count, axis=1, keepdims=True)
            targets[:, k * capacity : (k + 1) * capacity] = jnp.where(live, spot, -1)
            here = slice(k * capacity, (k + 1) * capacity)
            joined[here, :columns] = arrived[k][:capacity, :]
            lanes = iota((1, LANES), 1)
            if k < groups - 1:
                code = maps_ref[pl.ds(w * groups + (n ^ (k + 1)), 1), :]
            else:
                start = size + (k - groups + 1) * constraints
                code = jnp.where(lanes < constraints, lanes + start, -1).astype(f32)
            hot = (iota((width, LANES), 0).astype(f32) == code).astype(f32).astype(bf16)
            spread = dot(hot[:, :GROUP], arrived[k][capacity:, :])
            joined[here, columns:] = spread.T.astype(bf16)

    rows = iota((block, capacity), 0) + step * block
    hots = []
    for k in range(slots):
        target = targets[:, k * capacity : (k + 1) * capacity]
        hots.append((rows == target).astype(f32).astype(bf16))
    total = dot(jnp.concatenate(hots, axis=1), joined[...])
    early_ref[here_rows, :] = total[:, :columns]
    late_ref[here_rows, :] = total[:, columns:].astype(bf16)
    scaled = lane_scale_ref[...] * basis_ref[...].astype(f32)
    high = scaled.astype(bf16).astype(f32)
    start = size + 2 * constraints
    stop = start + 3 * constraints
    stack = jnp.concatenate(
        [jnp.zeros((start, block), f32), high, scaled - high, high, jnp.zeros((width - stop, block), f32)],
        axis=0,
    )
    own_ref[here_rows, :] = stack.T.astype(bf16)


def final_kernel(groups, size, constraints, part_ref, early_ref, late_ref, own_ref, *rest):
    pieces = rest[:groups]
    out_ref, values, highs, lows, owns = rest[groups:]
    _, n = place_of()

    @pl.when(pl.program_id(0) == 0)
    def _():
        c = pieces[0].shape[0]
        for k in range(groups):
            values[pl.ds(pl.multiple_of((n ^ k) * c, c), c), :] = pieces[k][...]
        value = values[...].T
        high = value.astype(bf16).astype(f32)
        low = value - high
        highs[...] = high.astype(bf16)
        lows[...] = low.astype(bf16)
        upper = iota(value.shape, 0) < size + 4 * constraints
        owns[...] = jnp.where(upper, high, low).astype(bf16)

    block = out_ref.shape[0]
    here = pl.ds(pl.multiple_of(pl.program_id(0) * block, block), block)
    late = late_ref[here, :]
    combined = (part_ref[here, :] + dot(own_ref[here, :], owns[...])).astype(bf16).astype(f32)
    out_ref[...] = combined + (early_ref[here, :] + (dot(late, highs[...]) + dot(late, lows[...])))


def body(
    residual,
    scaling,
    local_inverse,
    coarse_basis,
    primal_map,
    slot_index,
    slot_length,
    coarse_sub,
    coarse_pivot,
):
    slabs, groups = lax.axis_size("wide"), lax.axis_size("narrow")
    residual, inverse = residual[0, 0], local_inverse[0, 0]
    basis = coarse_basis[0, 0]
    slots, capacity = slot_index.shape[2] - 1, slot_index.shape[3]
    index = slot_index.reshape(slots + 1, 1, capacity)
    length = slot_length[0]
    size = coarse_sub.shape[1]
    order = ceil_lanes(size)
    rows, columns = residual.shape
    constraints = basis.shape[0]
    own_columns = columns // groups
    quarter = own_columns // 4
    width = ceil_lanes(size + 5 * constraints)
    scale = scaling[0, 0].reshape(rows // LANES, LANES)
    lane_scale = scaling[0]
    struct = jax.ShapeDtypeStruct

    def by_rows(block, cols):
        return pl.BlockSpec((block, cols), lambda i: (i, 0))

    def by_lanes(count, block):
        return pl.BlockSpec((count, block), lambda i: (0, i))

    any_space = pl.BlockSpec(memory_space=pl.ANY)
    vmem = pl.BlockSpec(memory_space=pltpu.VMEM)
    factors = [jnp.stack([coarse_sub, coarse_pivot], axis=1)]
    held, offsets, mask = factors[0], [0], slabs // 2
    while mask:
        factors.append(swap(held, "wide", mask))
        offsets = offsets + [o ^ mask for o in offsets]
        mask //= 2
        if mask:
            held = join(factors)

    sent = call(
        functools.partial(front_kernel, slabs, groups),
        struct((slabs * groups, quarter, LANES), f32),
        [any_space] * 4,
        (residual, scale, basis, primal_map[0]),
        out_specs=fixed((slabs * groups, quarter, LANES)),
        scratch=[
            pltpu.VMEM((rows, columns), bf16),
            pltpu.VMEM(scale.shape, f32),
            pltpu.VMEM(basis.shape, bf16),
            pltpu.VMEM(primal_map[0].shape, jnp.int32),
            pltpu.SemaphoreType.DMA((5,)),
        ],
        flops=2 * constraints * rows * columns,
        limit=63,
    )
    got = lax.all_to_all(sent, ("wide", "narrow"), split_axis=0, concat_axis=0, tiled=True)

    part, *outgoing = call(
        functools.partial(local_kernel, groups),
        [struct((rows, columns), f32)] + [struct((capacity + GROUP, columns), bf16)] * slots,
        [any_space] * 6,
        (inverse, residual, scale, lane_scale, basis, index),
        out_specs=[any_space] * (1 + slots),
        scratch=[pltpu.VMEM((capacity + GROUP, columns), bf16)] * slots
        + [
            pltpu.VMEM(lane_scale.shape, f32),
            pltpu.VMEM(basis.shape, bf16),
            pltpu.VMEM(index.shape, jnp.int32),
            pltpu.VMEM((rows, rows), bf16),
            pltpu.VMEM((rows, columns), bf16),
            pltpu.VMEM(scale.shape, f32),
            pltpu.VMEM((rows, columns), bf16),
            pltpu.VMEM((rows, columns), bf16),
            pltpu.VMEM((rows, columns), f32),
            pltpu.VMEM((constraints, rows), f32),
            pltpu.SemaphoreType.DMA((7,)),
            pltpu.SemaphoreType.DMA((2 + slots,)),
        ],
        flops=2 * rows * columns * (rows + slots * capacity),
        limit=57,
    )
    arrived = []
    for k in range(slots):
        if k < groups - 1:
            arrived.append(swap(outgoing[k], "narrow", k + 1))
        elif k == groups - 1:
            arrived.append(swap(outgoing[k], "wide", 1))
        else:
            arrived.append(swap_odd(outgoing[k], "wide"))

    right, maps = call(
        functools.partial(unpack_kernel, slabs, groups, constraints),
        [struct((slabs, own_columns, order), f32), struct((slabs * groups, LANES), f32)],
        [None],
        (got,),
        flops=2 * slabs * 3 * own_columns * LANES * order,
    )
    shares = call(
        functools.partial(solve_kernel, slabs, groups, constraints, offsets),
        [struct((own_columns, width), f32)] * groups,
        [None] * (2 + len(factors)),
        (right, maps, *factors),
        scratch=[
            pltpu.VMEM((2, slabs, order, order), f32),
            pltpu.VMEM((slabs, order, 2 * order), bf16),
            pltpu.VMEM((slabs, order, 2 * order), bf16),
            pltpu.VMEM((slabs, order, 2 * order), bf16),
            pltpu.VMEM((slabs, own_columns, order), f32),
        ],
        flops=2 * 3 * slabs * 2 * own_columns * order * 2 * order,
        limit=24 if slabs <= 8 else 62,
    )
    pieces = [shares[0]] + [swap(shares[k], "narrow", k) for k in range(1, groups)]

    block = min(rows, 1024)
    early, late, own = call(
        functools.partial(scatter_kernel, groups, size),
        [struct((rows, columns), f32), struct((rows, width), bf16), struct((rows, width), bf16)],
        [None, None, None, by_lanes(1, block), by_lanes(constraints, block)] + [None] * slots,
        (length, index, maps, lane_scale, basis, *arrived),
        grid=(rows // block,),
        out_specs=[vmem] * 3,
        scratch=[
            pltpu.VMEM((slots * capacity, columns + width), bf16),
            pltpu.VMEM((1, slots * capacity), jnp.int32),
        ],
        flops=2 * rows * slots * capacity * (columns + width),
    )
    result = call(
        functools.partial(final_kernel, groups, size, constraints),
        struct((rows, columns), f32),
        [vmem] * 4 + [None] * groups,
        (part, early, late, own, *pieces),
        grid=(rows // block,),
        out_specs=by_rows(block, columns),
        scratch=[
            pltpu.VMEM((columns, width), f32),
            pltpu.VMEM((width, columns), bf16),
            pltpu.VMEM((width, columns), bf16),
            pltpu.VMEM((width, columns), bf16),
        ],
        flops=2 * rows * columns * 3 * width,
    )
    return result[None, None]


def solution(mesh):
    in_specs = (
        P("wide", "narrow", None, None),
        P("wide", "narrow", None),
        P("wide", "narrow", None, None),
        P("wide", "narrow", None, None),
        P("wide", "narrow", None),
        P("wide", "narrow", None, None),
        P("wide", "narrow", None),
        P("wide", None, None),
        P("wide", None, None),
    )
    out_specs = P("wide", "narrow", None, None)

    return jax.shard_map(body, mesh=mesh, in_specs=in_specs, out_specs=out_specs, check_vma=False)
```

```python
import functools

import jax
import jax.numpy as jnp
from jax import lax
from jax.experimental import pallas as pl
from jax.experimental.pallas import tpu as pltpu
from jax.sharding import PartitionSpec as P


f32 = jnp.float32
bf16 = jnp.bfloat16
LANES = 128
GROUP = 32


def swap(block, axis, mask):
    count = lax.axis_size(axis)
    return lax.ppermute(block, axis, [(i, i ^ mask) for i in range(count)])


def swap_odd(block, axis):
    count = lax.axis_size(axis)
    pairs = [(i, i + 1) for i in range(1, count - 1, 2)]
    return lax.ppermute(block, axis, pairs + [(b, a) for a, b in pairs])


def ceil_lanes(size):
    return -(-size // LANES) * LANES


def iota(shape, axis):
    return lax.broadcasted_iota(jnp.int32, shape, axis)


def dot(left, right):
    return jnp.dot(left, right, preferred_element_type=f32)


def split_two(value):
    high = value.astype(bf16)
    return high, (value - high.astype(f32)).astype(bf16)


def split_three(value):
    high = value.astype(bf16)
    rest = value - high.astype(f32)
    middle = rest.astype(bf16)
    return high, middle, (rest - middle.astype(f32)).astype(bf16)


def turned_scale(scale_ref):
    scale = scale_ref[...]
    return jnp.concatenate(
        [scale, jnp.zeros((LANES - scale.shape[0], LANES), f32)], axis=0
    ).T


def call(kernel, outs, in_specs, args, grid=(1,), out_specs=None, scratch=(), flops=0, limit=24):
    many = isinstance(outs, (list, tuple))
    resident = pl.BlockSpec(memory_space=pltpu.VMEM)
    if out_specs is None:
        out_specs = [resident] * len(outs) if many else resident
    in_specs = [resident if s is None else s for s in in_specs]
    sizes = [a.size * a.dtype.itemsize for a in list(args) + (list(outs) if many else [outs])]
    return pl.pallas_call(
        kernel,
        out_shape=outs,
        grid=grid,
        in_specs=in_specs,
        out_specs=out_specs,
        scratch_shapes=list(scratch),
        compiler_params=pltpu.CompilerParams(vmem_limit_bytes=limit << 20),
        cost_estimate=pl.CostEstimate(flops=flops, bytes_accessed=sum(sizes), transcendentals=0),
    )(*args)


def join_kernel(*refs):
    start = 0
    for ref in refs[:-1]:
        refs[-1][start : start + ref.shape[0]] = ref[...]
        start += ref.shape[0]


def join(parts):
    total = sum(p.shape[0] for p in parts)
    out = jax.ShapeDtypeStruct((total,) + parts[0].shape[1:], parts[0].dtype)
    return call(join_kernel, out, [None] * len(parts), parts)


def copies(sources, targets, sems):
    moves = [pltpu.make_async_copy(a, b, sems.at[i]) for i, (a, b) in enumerate(zip(sources, targets))]
    for move in moves:
        move.start()
    return moves


def weigh(scale_turned, res_ref, start, count):
    for j in range(count // LANES):
        row = start + j * LANES
        factor = scale_turned[:, row // LANES : row // LANES + 1]
        yield (factor * res_ref[row : row + LANES, :].astype(f32)).astype(bf16)


def pack_pieces(slabs, groups, primal, map_ref, sent_ref):
    constraints, columns = primal.shape
    turned = jnp.concatenate([primal, jnp.zeros((LANES - constraints, columns), f32)], axis=0).T
    quarter = sent_ref.shape[1]
    spare = GROUP - constraints
    code = map_ref[...].astype(f32)
    code = jnp.concatenate([code, jnp.zeros((1, LANES - constraints), f32)], axis=1)
    lanes = iota((1, LANES), 1)
    tail = jnp.zeros((1, LANES), f32)
    for q in range(-(-constraints // spare)):
        start = GROUP * q + constraints
        inside = (lanes >= start) & (lanes < start + min(spare, constraints - spare * q))
        tail = jnp.where(inside, pltpu.roll(code, start - spare * q, 1), tail)
    tail = jnp.where(iota((quarter, LANES), 0) == 0, tail, 0.0)
    for m in range(groups):
        piece = tail
        for g in range(4):
            start = (m * 4 + g) * quarter
            part = turned[start : start + quarter, :]
            piece = piece + (pltpu.roll(part, GROUP * g, 1) if g else part)
        for v in range(slabs):
            sent_ref[v * groups + m] = piece


def place_of():
    return lax.axis_index("wide"), lax.axis_index("narrow")


def slot_rows(groups):
    w, n = place_of()
    parity = w & 1
    return [n ^ k for k in range(1, groups)] + [groups + 1 - parity, groups + parity]


def local_kernel(slabs, groups, inverse_any, res_any, scale_any, lane_scale_any, basis_any, index_any, map_any, sent_any, part_any, *rest):
    slots = groups + 1
    outs_any, outs = rest[:slots], rest[slots : 2 * slots]
    sent_ref, map_ref, lane_scale_ref, basis_ref, index_ref, inverse_ref, res_ref, scale_ref, weighted_ref, narrow_ref, part_ref, scaled_ref, sems, out_sems = rest[2 * slots :]
    rows = inverse_ref.shape[0]
    half = rows // 2
    halves = [pl.ds(i * half, half) for i in range(2)]
    sources = [scale_any, res_any, basis_any, map_any, lane_scale_any, index_any]
    targets = [scale_ref, res_ref, basis_ref, map_ref, lane_scale_ref, index_ref]
    sources += [inverse_any.at[p] for p in halves]
    targets += [inverse_ref.at[p] for p in halves]
    moves = copies(sources, targets, sems)
    for move in moves[:6]:
        move.wait()
    turned = turned_scale(scale_ref)
    for j, value in enumerate(weigh(turned, res_ref, 0, rows)):
        weighted_ref[j * LANES : (j + 1) * LANES, :] = value
    pack_pieces(slabs, groups, dot(basis_ref[...], weighted_ref[...]), map_ref, sent_ref)
    leaving = [pltpu.make_async_copy(sent_ref, sent_any, out_sems.at[2 + slots])]
    leaving[0].start()
    capacity = index_ref.shape[2]
    constraints = basis_ref.shape[0]
    picks = [index_ref[r] for r in slot_rows(groups)]
    scaled_ref[...] = lane_scale_ref[...] * basis_ref[...].astype(f32)
    for k in range(slots):
        parts = []
        for c in range(capacity // LANES):
            spot = jnp.broadcast_to(picks[k][:, c * LANES : (c + 1) * LANES], (constraints, LANES))
            inner, outer = spot & (LANES - 1), spot // LANES
            value = jnp.zeros((constraints, LANES), f32)
            for j in range(rows // LANES):
                found = jnp.take_along_axis(scaled_ref[:, j * LANES : (j + 1) * LANES], inner, axis=1)
                value = jnp.where(outer == j, found, value)
            parts.append(value)
        fill = jnp.zeros((GROUP - constraints, capacity), f32)
        outs[k][capacity:, :] = jnp.concatenate([jnp.concatenate(parts, axis=1), fill], axis=0).astype(bf16)
    for i, p in enumerate(halves):
        moves[6 + i].wait()
        block = min(half, 256)
        for start in range(i * half, (i + 1) * half, block):
            part = dot(inverse_ref[start : start + block, :], weighted_ref[...])
            for j in range(block // LANES):
                row = start + j * LANES
                column = row // LANES
                scaled = turned[:, column : column + 1] * part[j * LANES : (j + 1) * LANES, :]
                part_ref[row : row + LANES, :] = scaled
                narrow_ref[row : row + LANES, :] = scaled.astype(bf16)
        leave = pltpu.make_async_copy(part_ref.at[p], part_any.at[p], out_sems.at[i])
        leave.start()
        leaving.append(leave)
    spare_rows = [jnp.zeros((LANES - slots, capacity), jnp.int32)]
    columns_of = jnp.concatenate(picks + spare_rows, axis=0).astype(f32).T
    lanes = iota((capacity, LANES), 1).astype(f32)
    for k in range(slots):
        spot = jnp.broadcast_to(columns_of[:, k : k + 1], (capacity, LANES))
        hots = [(spot == lanes + float(j * LANES)).astype(f32).astype(bf16) for j in range(rows // LANES)]
        outs[k][:capacity, :] = dot(jnp.concatenate(hots, axis=1), narrow_ref[...]).astype(bf16)
        leave = pltpu.make_async_copy(outs[k], outs_any[k], out_sems.at[2 + k])
        leave.start()
        leaving.append(leave)
    for leave in leaving:
        leave.wait()


def unpack_kernel(slabs, groups, constraints, got_ref, right_ref, maps_ref):
    pieces, quarter, _ = got_ref.shape
    spare = GROUP - constraints
    heads = jnp.concatenate([got_ref[i, 0:1, :] for i in range(pieces)], axis=0)
    lanes = iota((pieces, LANES), 1)
    maps = jnp.full((pieces, LANES), -1.0, f32)
    for q in range(-(-constraints // spare)):
        shift = (spare * q - GROUP * q - constraints) % LANES
        moved = pltpu.roll(heads, shift, 1) if shift else heads
        inside = (lanes >= spare * q) & (lanes < min(spare * (q + 1), constraints))
        maps = jnp.where(inside, moved, maps)
    maps_ref[...] = maps
    order = right_ref.shape[2]
    halves = groups * GROUP // LANES
    lanes = iota((quarter, LANES), 1) // GROUP
    wide = iota((1, LANES), 1) // GROUP

    def one(v, carry):
        value, codes = [], []
        for h in range(halves):
            rows = []
            for g in range(4):
                row = None
                for j in range(4):
                    part = got_ref[v * groups + 4 * h + j]
                    shift = (GROUP * (j - g)) % LANES
                    part = pltpu.roll(part, shift, 1) if shift else part
                    row = part if row is None else jnp.where(lanes == j, part, row)
                rows.append(row)
            value.append(jnp.concatenate(rows, axis=0))
            code = None
            for j in range(4):
                part = maps_ref[pl.ds(v * groups + 4 * h + j, 1), :]
                part = pltpu.roll(part, GROUP * j, 1) if j else part
                code = part if code is None else jnp.where(wide == j, part, code)
            codes.append(code)
        value = jnp.concatenate(value, axis=1) if halves > 1 else value[0]
        code = jnp.concatenate(codes, axis=1) if halves > 1 else codes[0]
        hot = (iota((order, halves * LANES), 0).astype(f32) == code).astype(f32).astype(bf16)
        stacked = jnp.concatenate(split_three(value), axis=0)
        total = lax.dot_general(stacked, hot, (((1,), (1,)), ((), ())), preferred_element_type=f32)
        c = value.shape[0]
        right_ref[v] = total[:c] + total[c : 2 * c] + total[2 * c :]
        return carry

    lax.fori_loop(0, slabs, one, 0, unroll=slabs <= 8)


def solve_kernel(slabs, groups, constraints, offsets, right_ref, maps_ref, *rest):
    mine, other, shares = rest[:2], rest[2:4], rest[4 : 4 + groups]
    raw, forward, backward, pivots, solved = rest[4 + groups :]
    w, n = place_of()
    core = n & 1
    size = mine[0].shape[2]
    order = raw.shape[2]
    if size != order:
        raw[...] = jnp.zeros_like(raw)
    start = 0
    for a, b in zip(mine, other):
        for i in range(a.shape[0]):
            slab = w ^ offsets[start + i]
            raw[core, slab, :size, :size] = a[i]
            raw[1 - core, slab, :size, :size] = b[i]
        start += a.shape[0]
    c = right_ref.shape[1]
    few = slabs <= 8

    def prepare(v, carry):
        sub = raw[0, v]
        for ref, value in ((forward, sub.T), (backward, sub), (pivots, raw[1, v])):
            high, low = split_two(value)
            ref[v, :, :order] = high
            ref[v, :, order:] = low
        return carry

    def times(value, factor):
        total = dot(jnp.concatenate(split_two(value), axis=0), factor)
        return total[:c, :order] + (total[:c, order:] + total[c:, :order])

    def down(v, value):
        value = right_ref[v] - times(value, forward[v])
        solved[v] = value
        return value

    def pivot(v, carry):
        solved[v] = times(solved[v], pivots[v])
        return carry

    def up(i, value):
        v = slabs - 2 - i
        value = solved[v] - times(value, backward[v + 1])
        solved[v] = value
        return value

    lax.fori_loop(0, slabs, prepare, 0, unroll=few)
    solved[0] = right_ref[0]
    lax.fori_loop(1, slabs, down, right_ref[0], unroll=few)
    lax.fori_loop(0, slabs, pivot, 0, unroll=few)
    lax.fori_loop(0, slabs - 1, up, solved[slabs - 1], unroll=few)

    parity = w & 1
    sides = [w, w ^ 1, jnp.clip(w - 1 + 2 * parity, 0, slabs - 1)]
    value = jnp.concatenate([solved[s] for s in sides], axis=1)
    stacked = jnp.concatenate(split_three(value), axis=0)
    width = shares[0].shape[1]
    lanes = iota((1, width), 1)
    rows = iota((order, width), 0).astype(f32)
    starts = [
        [size + (2 + i) * constraints for i in range(3)],
        [size],
        [size + constraints],
    ]
    for k in range(groups):
        hots = []
        for s, (side, places) in enumerate(zip(sides, starts)):
            code = maps_ref[pl.ds(side * groups + (n ^ k), 1), :]
            code = jnp.concatenate([code, jnp.full((1, width - LANES), -1.0, f32)], axis=1)
            full = jnp.where(lanes < size, lanes.astype(f32), -1.0) if s == 0 else jnp.full((1, width), -1.0, f32)
            for place in places:
                inside = (lanes >= place) & (lanes < place + constraints)
                full = jnp.where(inside, pltpu.roll(code, place, 1), full)
            hots.append((rows == full).astype(f32).astype(bf16))
        total = dot(stacked, jnp.concatenate(hots, axis=0))
        shares[k][...] = total[:c] + total[c : 2 * c] + total[2 * c :]


def scatter_kernel(groups, size, length_ref, index_ref, maps_ref, lane_scale_ref, basis_ref, *rest):
    slots = groups + 1
    arrived = rest[:slots]
    early_ref, late_ref, own_ref, joined, targets = rest[slots:]
    step = pl.program_id(0)
    columns, width = early_ref.shape[1], late_ref.shape[1]
    block = early_ref.shape[0] // pl.num_programs(0)
    here_rows = pl.ds(pl.multiple_of(step * block, block), block)
    constraints = basis_ref.shape[0]
    capacity = index_ref.shape[2]
    w, n = place_of()

    @pl.when(step == 0)
    def _():
        for k, r in enumerate(slot_rows(groups)):
            spot = index_ref[r]
            count = jnp.where(iota(length_ref.shape, 1) == r, length_ref[...], 0)
            live = iota((1, capacity), 1) < jnp.sum(count, axis=1, keepdims=True)
            targets[:, k * capacity : (k + 1) * capacity] = jnp.where(live, spot, -1)
            here = slice(k * capacity, (k + 1) * capacity)
            joined[here, :columns] = arrived[k][:capacity, :]
            lanes = iota((1, LANES), 1)
            if k < groups - 1:
                code = maps_ref[pl.ds(w * groups + (n ^ (k + 1)), 1), :]
            else:
                start = size + (k - groups + 1) * constraints
                code = jnp.where(lanes < constraints, lanes + start, -1).astype(f32)
            hot = (iota((width, LANES), 0).astype(f32) == code).astype(f32).astype(bf16)
            spread = dot(hot[:, :GROUP], arrived[k][capacity:, :])
            joined[here, columns:] = spread.T.astype(bf16)

    rows = iota((block, capacity), 0) + step * block
    hots = []
    for k in range(slots):
        target = targets[:, k * capacity : (k + 1) * capacity]
        hots.append((rows == target).astype(f32).astype(bf16))
    total = dot(jnp.concatenate(hots, axis=1), joined[...])
    early_ref[here_rows, :] = total[:, :columns]
    late_ref[here_rows, :] = total[:, columns:].astype(bf16)
    scaled = lane_scale_ref[...] * basis_ref[...].astype(f32)
    high = scaled.astype(bf16).astype(f32)
    start = size + 2 * constraints
    stop = start + 3 * constraints
    stack = jnp.concatenate(
        [jnp.zeros((start, block), f32), high, scaled - high, high, jnp.zeros((width - stop, block), f32)],
        axis=0,
    )
    own_ref[here_rows, :] = stack.T.astype(bf16)


def final_kernel(groups, size, constraints, part_ref, early_ref, late_ref, own_ref, *rest):
    pieces = rest[:groups]
    out_ref, values, highs, lows, owns = rest[groups:]
    _, n = place_of()

    @pl.when(pl.program_id(0) == 0)
    def _():
        c = pieces[0].shape[0]
        for k in range(groups):
            values[pl.ds(pl.multiple_of((n ^ k) * c, c), c), :] = pieces[k][...]
        value = values[...].T
        high = value.astype(bf16).astype(f32)
        low = value - high
        highs[...] = high.astype(bf16)
        lows[...] = low.astype(bf16)
        upper = iota(value.shape, 0) < size + 4 * constraints
        owns[...] = jnp.where(upper, high, low).astype(bf16)

    block = out_ref.shape[0]
    here = pl.ds(pl.multiple_of(pl.program_id(0) * block, block), block)
    late = late_ref[here, :]
    combined = (part_ref[here, :] + dot(own_ref[here, :], owns[...])).astype(bf16).astype(f32)
    out_ref[...] = combined + (early_ref[here, :] + (dot(late, highs[...]) + dot(late, lows[...])))


def body(
    residual,
    scaling,
    local_inverse,
    coarse_basis,
    primal_map,
    slot_index,
    slot_length,
    coarse_sub,
    coarse_pivot,
):
    slabs, groups = lax.axis_size("wide"), lax.axis_size("narrow")
    residual, inverse = residual[0, 0], local_inverse[0, 0]
    basis = coarse_basis[0, 0]
    slots, capacity = slot_index.shape[2] - 1, slot_index.shape[3]
    index = slot_index.reshape(slots + 1, 1, capacity)
    length = slot_length[0]
    size = coarse_sub.shape[1]
    order = ceil_lanes(size)
    rows, columns = residual.shape
    constraints = basis.shape[0]
    own_columns = columns // groups
    quarter = own_columns // 4
    width = ceil_lanes(size + 5 * constraints)
    scale = scaling[0, 0].reshape(rows // LANES, LANES)
    lane_scale = scaling[0]
    struct = jax.ShapeDtypeStruct

    def by_rows(block, cols):
        return pl.BlockSpec((block, cols), lambda i: (i, 0))

    def by_lanes(count, block):
        return pl.BlockSpec((count, block), lambda i: (0, i))

    any_space = pl.BlockSpec(memory_space=pl.ANY)
    vmem = pl.BlockSpec(memory_space=pltpu.VMEM)
    n = lax.axis_index("narrow")
    factors = [jnp.where((n & 1) == 0, coarse_sub, coarse_pivot)]
    held, offsets = factors[0], [0]
    masks = [1 << i for i in reversed(range(slabs.bit_length() - 1))]
    masks[-2:] = masks[:-3:-1]
    for mask in masks:
        factors.append(swap(held, "wide", mask))
        offsets = offsets + [o ^ mask for o in offsets]
        if len(offsets) < slabs:
            held = join(factors)

    mine, other = [held, factors[-1]], []
    for piece in mine:
        other.append(swap(piece, "narrow", 1))

    sent, part, *outgoing = call(
        functools.partial(local_kernel, slabs, groups),
        [struct((slabs * groups, quarter, LANES), f32), struct((rows, columns), f32)]
        + [struct((capacity + GROUP, columns), bf16)] * slots,
        [any_space] * 7,
        (inverse, residual, scale, lane_scale, basis, index, primal_map[0]),
        out_specs=[any_space] * (2 + slots),
        scratch=[pltpu.VMEM((capacity + GROUP, columns), bf16)] * slots
        + [
            pltpu.VMEM((slabs * groups, quarter, LANES), f32),
            pltpu.VMEM(primal_map[0].shape, jnp.int32),
            pltpu.VMEM(lane_scale.shape, f32),
            pltpu.VMEM(basis.shape, bf16),
            pltpu.VMEM(index.shape, jnp.int32),
            pltpu.VMEM((rows, rows), bf16),
            pltpu.VMEM((rows, columns), bf16),
            pltpu.VMEM(scale.shape, f32),
            pltpu.VMEM((rows, columns), bf16),
            pltpu.VMEM((rows, columns), bf16),
            pltpu.VMEM((rows, columns), f32),
            pltpu.VMEM((constraints, rows), f32),
            pltpu.SemaphoreType.DMA((8,)),
            pltpu.SemaphoreType.DMA((3 + slots,)),
        ],
        flops=2 * rows * columns * (rows + slots * capacity),
        limit=57,
    )
    got = lax.all_to_all(sent, ("wide", "narrow"), split_axis=0, concat_axis=0, tiled=True)
    arrived = []
    for k in range(slots):
        if k < groups - 1:
            arrived.append(swap(outgoing[k], "narrow", k + 1))
        elif k == groups - 1:
            arrived.append(swap(outgoing[k], "wide", 1))
        else:
            arrived.append(swap_odd(outgoing[k], "wide"))

    right, maps = call(
        functools.partial(unpack_kernel, slabs, groups, constraints),
        [struct((slabs, own_columns, order), f32), struct((slabs * groups, LANES), f32)],
        [None],
        (got,),
        flops=2 * slabs * 3 * own_columns * LANES * order,
    )
    shares = call(
        functools.partial(solve_kernel, slabs, groups, constraints, offsets),
        [struct((own_columns, width), f32)] * groups,
        [None] * (2 + len(mine) + len(other)),
        (right, maps, *mine, *other),
        scratch=[
            pltpu.VMEM((2, slabs, order, order), f32),
            pltpu.VMEM((slabs, order, 2 * order), bf16),
            pltpu.VMEM((slabs, order, 2 * order), bf16),
            pltpu.VMEM((slabs, order, 2 * order), bf16),
            pltpu.VMEM((slabs, own_columns, order), f32),
        ],
        flops=2 * 3 * slabs * 2 * own_columns * order * 2 * order,
        limit=24 if slabs <= 8 else 62,
    )
    pieces = [shares[0]] + [swap(shares[k], "narrow", k) for k in range(1, groups)]

    block = min(rows, 1024)
    early, late, own = call(
        functools.partial(scatter_kernel, groups, size),
        [struct((rows, columns), f32), struct((rows, width), bf16), struct((rows, width), bf16)],
        [None, None, None, by_lanes(1, block), by_lanes(constraints, block)] + [None] * slots,
        (length, index, maps, lane_scale, basis, *arrived),
        grid=(rows // block,),
        out_specs=[vmem] * 3,
        scratch=[
            pltpu.VMEM((slots * capacity, columns + width), bf16),
            pltpu.VMEM((1, slots * capacity), jnp.int32),
        ],
        flops=2 * rows * slots * capacity * (columns + width),
    )
    result = call(
        functools.partial(final_kernel, groups, size, constraints),
        struct((rows, columns), f32),
        [vmem] * 4 + [None] * groups,
        (part, early, late, own, *pieces),
        grid=(rows // block,),
        out_specs=by_rows(block, columns),
        scratch=[
            pltpu.VMEM((columns, width), f32),
            pltpu.VMEM((width, columns), bf16),
            pltpu.VMEM((width, columns), bf16),
            pltpu.VMEM((width, columns), bf16),
        ],
        flops=2 * rows * columns * 3 * width,
    )
    return result[None, None]


def solution(mesh):
    in_specs = (
        P("wide", "narrow", None, None),
        P("wide", "narrow", None),
        P("wide", "narrow", None, None),
        P("wide", "narrow", None, None),
        P("wide", "narrow", None),
        P("wide", "narrow", None, None),
        P("wide", "narrow", None),
        P("wide", None, None),
        P("wide", None, None),
    )
    out_specs = P("wide", "narrow", None, None)

    return jax.shard_map(body, mesh=mesh, in_specs=in_specs, out_specs=out_specs, check_vma=False)
```

```python
import functools

import jax
import jax.numpy as jnp
from jax import lax
from jax.experimental import pallas as pl
from jax.experimental.pallas import tpu as pltpu
from jax.sharding import PartitionSpec as P


f32 = jnp.float32
bf16 = jnp.bfloat16
LANES = 128
GROUP = 32


def swap(block, axis, mask):
    count = lax.axis_size(axis)
    return lax.ppermute(block, axis, [(i, i ^ mask) for i in range(count)])


def swap_odd(block, axis):
    count = lax.axis_size(axis)
    pairs = [(i, i + 1) for i in range(1, count - 1, 2)]
    return lax.ppermute(block, axis, pairs + [(b, a) for a, b in pairs])


def ceil_lanes(size):
    return -(-size // LANES) * LANES


def iota(shape, axis):
    return lax.broadcasted_iota(jnp.int32, shape, axis)


def dot(left, right):
    return jnp.dot(left, right, preferred_element_type=f32)


def split_two(value):
    high = value.astype(bf16)
    return high, (value - high.astype(f32)).astype(bf16)


def split_three(value):
    high = value.astype(bf16)
    rest = value - high.astype(f32)
    middle = rest.astype(bf16)
    return high, middle, (rest - middle.astype(f32)).astype(bf16)


def turned_scale(scale_ref):
    scale = scale_ref[...]
    return jnp.concatenate(
        [scale, jnp.zeros((LANES - scale.shape[0], LANES), f32)], axis=0
    ).T


def call(kernel, outs, in_specs, args, grid=(1,), out_specs=None, scratch=(), flops=0, limit=24):
    many = isinstance(outs, (list, tuple))
    resident = pl.BlockSpec(memory_space=pltpu.VMEM)
    if out_specs is None:
        out_specs = [resident] * len(outs) if many else resident
    in_specs = [resident if s is None else s for s in in_specs]
    sizes = [a.size * a.dtype.itemsize for a in list(args) + (list(outs) if many else [outs])]
    return pl.pallas_call(
        kernel,
        out_shape=outs,
        grid=grid,
        in_specs=in_specs,
        out_specs=out_specs,
        scratch_shapes=list(scratch),
        compiler_params=pltpu.CompilerParams(vmem_limit_bytes=limit << 20),
        cost_estimate=pl.CostEstimate(flops=flops, bytes_accessed=sum(sizes), transcendentals=0),
    )(*args)


def join_kernel(*refs):
    start = 0
    for ref in refs[:-1]:
        refs[-1][start : start + ref.shape[0]] = ref[...]
        start += ref.shape[0]


def join(parts):
    total = sum(p.shape[0] for p in parts)
    out = jax.ShapeDtypeStruct((total,) + parts[0].shape[1:], parts[0].dtype)
    return call(join_kernel, out, [None] * len(parts), parts)


def copies(sources, targets, sems):
    moves = [pltpu.make_async_copy(a, b, sems.at[i]) for i, (a, b) in enumerate(zip(sources, targets))]
    for move in moves:
        move.start()
    return moves


def weigh(scale_turned, res_ref, start, count):
    for j in range(count // LANES):
        row = start + j * LANES
        factor = scale_turned[:, row // LANES : row // LANES + 1]
        yield (factor * res_ref[row : row + LANES, :].astype(f32)).astype(bf16)


def pack_pieces(slabs, groups, primal, map_ref, sent_ref):
    constraints, columns = primal.shape
    turned = jnp.concatenate([primal, jnp.zeros((LANES - constraints, columns), f32)], axis=0).T
    quarter = sent_ref.shape[1]
    spare = GROUP - constraints
    code = map_ref[...].astype(f32)
    code = jnp.concatenate([code, jnp.zeros((1, LANES - constraints), f32)], axis=1)
    lanes = iota((1, LANES), 1)
    tail = jnp.zeros((1, LANES), f32)
    for q in range(-(-constraints // spare)):
        start = GROUP * q + constraints
        inside = (lanes >= start) & (lanes < start + min(spare, constraints - spare * q))
        tail = jnp.where(inside, pltpu.roll(code, start - spare * q, 1), tail)
    tail = jnp.where(iota((quarter, LANES), 0) == 0, tail, 0.0)
    for m in range(groups):
        piece = tail
        for g in range(4):
            start = (m * 4 + g) * quarter
            part = turned[start : start + quarter, :]
            piece = piece + (pltpu.roll(part, GROUP * g, 1) if g else part)
        for v in range(slabs):
            sent_ref[v * groups + m] = piece


def place_of():
    return lax.axis_index("wide"), lax.axis_index("narrow")


def slot_rows(groups):
    w, n = place_of()
    parity = w & 1
    return [n ^ k for k in range(1, groups)] + [groups + 1 - parity, groups + parity]


def local_kernel(slabs, groups, inverse_any, res_any, scale_any, lane_scale_any, basis_any, index_any, map_any, sent_any, part_any, *rest):
    slots = groups + 1
    outs_any, outs = rest[:slots], rest[slots : 2 * slots]
    sent_ref, map_ref, lane_scale_ref, basis_ref, index_ref, inverse_ref, res_ref, scale_ref, weighted_ref, narrow_ref, part_ref, scaled_ref, first_ref, sems, out_sems = rest[2 * slots :]
    rows = inverse_ref.shape[0]
    half = rows // 2
    halves = [pl.ds(i * half, half) for i in range(2)]
    sources = [scale_any, res_any, basis_any, map_any, lane_scale_any, index_any]
    targets = [scale_ref, res_ref, basis_ref, map_ref, lane_scale_ref, index_ref]
    sources += [inverse_any.at[p] for p in halves]
    targets += [inverse_ref.at[p] for p in halves]
    moves = copies(sources, targets, sems)
    for move in moves[:6]:
        move.wait()
    turned = turned_scale(scale_ref)
    for j, value in enumerate(weigh(turned, res_ref, 0, rows)):
        weighted_ref[j * LANES : (j + 1) * LANES, :] = value
    pack_pieces(slabs, groups, dot(basis_ref[...], weighted_ref[...]), map_ref, sent_ref)
    leaving = [pltpu.make_async_copy(sent_ref, sent_any, out_sems.at[2 + slots])]
    leaving[0].start()
    capacity = index_ref.shape[2]
    constraints = basis_ref.shape[0]
    picks = [index_ref[r] for r in slot_rows(groups)]
    scaled_ref[...] = lane_scale_ref[...] * basis_ref[...].astype(f32)
    for k in range(slots):
        parts = []
        for c in range(capacity // LANES):
            spot = jnp.broadcast_to(picks[k][:, c * LANES : (c + 1) * LANES], (constraints, LANES))
            inner, outer = spot & (LANES - 1), spot // LANES
            value = jnp.zeros((constraints, LANES), f32)
            for j in range(rows // LANES):
                found = jnp.take_along_axis(scaled_ref[:, j * LANES : (j + 1) * LANES], inner, axis=1)
                value = jnp.where(outer == j, found, value)
            parts.append(value)
        fill = jnp.zeros((GROUP - constraints, capacity), f32)
        outs[k][capacity:, :] = jnp.concatenate([jnp.concatenate(parts, axis=1), fill], axis=0).astype(bf16)
    spare_rows = [jnp.zeros((LANES - slots, capacity), jnp.int32)]
    columns_of = jnp.concatenate(picks + spare_rows, axis=0).astype(f32).T
    lanes = iota((capacity, LANES), 1).astype(f32)
    for i, p in enumerate(halves):
        moves[6 + i].wait()
        block = min(half, 256)
        for start in range(i * half, (i + 1) * half, block):
            part = dot(inverse_ref[start : start + block, :], weighted_ref[...])
            for j in range(block // LANES):
                row = start + j * LANES
                column = row // LANES
                scaled = turned[:, column : column + 1] * part[j * LANES : (j + 1) * LANES, :]
                part_ref[row : row + LANES, :] = scaled
                narrow_ref[row : row + LANES, :] = scaled.astype(bf16)
        leave = pltpu.make_async_copy(part_ref.at[p], part_any.at[p], out_sems.at[i])
        leave.start()
        leaving.append(leave)
        for k in range(slots):
            spot = jnp.broadcast_to(columns_of[:, k : k + 1], (capacity, LANES))
            hots = [
                (spot == lanes + float(j * LANES)).astype(f32).astype(bf16)
                for j in range(i * half // LANES, (i + 1) * half // LANES)
            ]
            found = dot(jnp.concatenate(hots, axis=1), narrow_ref[i * half : (i + 1) * half, :])
            if i == 0:
                first_ref[k] = found
                continue
            outs[k][:capacity, :] = (first_ref[k] + found).astype(bf16)
            leave = pltpu.make_async_copy(outs[k], outs_any[k], out_sems.at[2 + k])
            leave.start()
            leaving.append(leave)
    for leave in leaving:
        leave.wait()


def unpack_kernel(slabs, groups, constraints, got_ref, right_ref, maps_ref):
    pieces, quarter, _ = got_ref.shape
    spare = GROUP - constraints
    heads = jnp.concatenate([got_ref[i, 0:1, :] for i in range(pieces)], axis=0)
    lanes = iota((pieces, LANES), 1)
    maps = jnp.full((pieces, LANES), -1.0, f32)
    for q in range(-(-constraints // spare)):
        shift = (spare * q - GROUP * q - constraints) % LANES
        moved = pltpu.roll(heads, shift, 1) if shift else heads
        inside = (lanes >= spare * q) & (lanes < min(spare * (q + 1), constraints))
        maps = jnp.where(inside, moved, maps)
    maps_ref[...] = maps
    order = right_ref.shape[2]
    halves = groups * GROUP // LANES
    lanes = iota((quarter, LANES), 1) // GROUP
    wide = iota((1, LANES), 1) // GROUP

    def one(v, carry):
        value, codes = [], []
        for h in range(halves):
            rows = []
            for g in range(4):
                row = None
                for j in range(4):
                    part = got_ref[v * groups + 4 * h + j]
                    shift = (GROUP * (j - g)) % LANES
                    part = pltpu.roll(part, shift, 1) if shift else part
                    row = part if row is None else jnp.where(lanes == j, part, row)
                rows.append(row)
            value.append(jnp.concatenate(rows, axis=0))
            code = None
            for j in range(4):
                part = maps_ref[pl.ds(v * groups + 4 * h + j, 1), :]
                part = pltpu.roll(part, GROUP * j, 1) if j else part
                code = part if code is None else jnp.where(wide == j, part, code)
            codes.append(code)
        value = jnp.concatenate(value, axis=1) if halves > 1 else value[0]
        code = jnp.concatenate(codes, axis=1) if halves > 1 else codes[0]
        hot = (iota((order, halves * LANES), 0).astype(f32) == code).astype(f32).astype(bf16)
        stacked = jnp.concatenate(split_three(value), axis=0)
        total = lax.dot_general(stacked, hot, (((1,), (1,)), ((), ())), preferred_element_type=f32)
        c = value.shape[0]
        right_ref[v] = total[:c] + total[c : 2 * c] + total[2 * c :]
        return carry

    lax.fori_loop(0, slabs, one, 0, unroll=slabs <= 8)


def solve_kernel(slabs, groups, constraints, offsets, right_ref, maps_ref, *rest):
    mine, other, shares = rest[:2], rest[2:4], rest[4 : 4 + groups]
    raw, forward, backward, pivots, solved = rest[4 + groups :]
    w, n = place_of()
    core = n & 1
    size = mine[0].shape[2]
    order = raw.shape[2]
    if size != order:
        raw[...] = jnp.zeros_like(raw)
    start = 0
    for a, b in zip(mine, other):
        for i in range(a.shape[0]):
            slab = w ^ offsets[start + i]
            raw[core, slab, :size, :size] = a[i]
            raw[1 - core, slab, :size, :size] = b[i]
        start += a.shape[0]
    c = right_ref.shape[1]
    few = slabs <= 8

    def prepare(v, carry):
        sub = raw[0, v]
        for ref, value in ((forward, sub.T), (backward, sub), (pivots, raw[1, v])):
            high, low = split_two(value)
            ref[v, :, :order] = high
            ref[v, :, order:] = low
        return carry

    def times(value, factor):
        total = dot(jnp.concatenate(split_two(value), axis=0), factor)
        return total[:c, :order] + (total[:c, order:] + total[c:, :order])

    def down(v, value):
        value = right_ref[v] - times(value, forward[v])
        solved[v] = value
        return value

    def pivot(v, carry):
        solved[v] = times(solved[v], pivots[v])
        return carry

    def up(i, value):
        v = slabs - 2 - i
        value = solved[v] - times(value, backward[v + 1])
        solved[v] = value
        return value

    lax.fori_loop(0, slabs, prepare, 0, unroll=few)
    solved[0] = right_ref[0]
    lax.fori_loop(1, slabs, down, right_ref[0], unroll=few)
    lax.fori_loop(0, slabs, pivot, 0, unroll=few)
    lax.fori_loop(0, slabs - 1, up, solved[slabs - 1], unroll=few)

    parity = w & 1
    sides = [w, w ^ 1, jnp.clip(w - 1 + 2 * parity, 0, slabs - 1)]
    value = jnp.concatenate([solved[s] for s in sides], axis=1)
    stacked = jnp.concatenate(split_three(value), axis=0)
    width = shares[0].shape[1]
    lanes = iota((1, width), 1)
    rows = iota((order, width), 0).astype(f32)
    starts = [
        [size + (2 + i) * constraints for i in range(3)],
        [size],
        [size + constraints],
    ]
    for k in range(groups):
        hots = []
        for s, (side, places) in enumerate(zip(sides, starts)):
            code = maps_ref[pl.ds(side * groups + (n ^ k), 1), :]
            code = jnp.concatenate([code, jnp.full((1, width - LANES), -1.0, f32)], axis=1)
            full = jnp.where(lanes < size, lanes.astype(f32), -1.0) if s == 0 else jnp.full((1, width), -1.0, f32)
            for place in places:
                inside = (lanes >= place) & (lanes < place + constraints)
                full = jnp.where(inside, pltpu.roll(code, place, 1), full)
            hots.append((rows == full).astype(f32).astype(bf16))
        total = dot(stacked, jnp.concatenate(hots, axis=0))
        shares[k][...] = total[:c] + total[c : 2 * c] + total[2 * c :]


def scatter_kernel(groups, size, length_ref, index_ref, maps_ref, lane_scale_ref, basis_ref, *rest):
    slots = groups + 1
    arrived = rest[:slots]
    early_ref, late_ref, own_ref, joined, targets = rest[slots:]
    step = pl.program_id(0)
    columns, width = early_ref.shape[1], late_ref.shape[1]
    block = early_ref.shape[0] // pl.num_programs(0)
    here_rows = pl.ds(pl.multiple_of(step * block, block), block)
    constraints = basis_ref.shape[0]
    capacity = index_ref.shape[2]
    w, n = place_of()

    @pl.when(step == 0)
    def _():
        for k, r in enumerate(slot_rows(groups)):
            spot = index_ref[r]
            count = jnp.where(iota(length_ref.shape, 1) == r, length_ref[...], 0)
            live = iota((1, capacity), 1) < jnp.sum(count, axis=1, keepdims=True)
            targets[:, k * capacity : (k + 1) * capacity] = jnp.where(live, spot, -1)
            here = slice(k * capacity, (k + 1) * capacity)
            joined[here, :columns] = arrived[k][:capacity, :]
            lanes = iota((1, LANES), 1)
            if k < groups - 1:
                code = maps_ref[pl.ds(w * groups + (n ^ (k + 1)), 1), :]
            else:
                start = size + (k - groups + 1) * constraints
                code = jnp.where(lanes < constraints, lanes + start, -1).astype(f32)
            hot = (iota((width, LANES), 0).astype(f32) == code).astype(f32).astype(bf16)
            spread = dot(hot[:, :GROUP], arrived[k][capacity:, :])
            joined[here, columns:] = spread.T.astype(bf16)

    rows = iota((block, capacity), 0) + step * block
    hots = []
    for k in range(slots):
        target = targets[:, k * capacity : (k + 1) * capacity]
        hots.append((rows == target).astype(f32).astype(bf16))
    total = dot(jnp.concatenate(hots, axis=1), joined[...])
    early_ref[here_rows, :] = total[:, :columns]
    late_ref[here_rows, :] = total[:, columns:].astype(bf16)
    scaled = lane_scale_ref[...] * basis_ref[...].astype(f32)
    high = scaled.astype(bf16).astype(f32)
    start = size + 2 * constraints
    stop = start + 3 * constraints
    stack = jnp.concatenate(
        [jnp.zeros((start, block), f32), high, scaled - high, high, jnp.zeros((width - stop, block), f32)],
        axis=0,
    )
    own_ref[here_rows, :] = stack.T.astype(bf16)


def final_kernel(groups, size, constraints, part_ref, early_ref, late_ref, own_ref, *rest):
    pieces = rest[:groups]
    out_any, out_ref, values, highs, lows, owns, sems = rest[groups:]
    _, n = place_of()
    c = pieces[0].shape[0]
    for k in range(groups):
        values[pl.ds(pl.multiple_of((n ^ k) * c, c), c), :] = pieces[k][...]
    value = values[...].T
    high = value.astype(bf16).astype(f32)
    low = value - high
    highs[...] = high.astype(bf16)
    lows[...] = low.astype(bf16)
    upper = iota(value.shape, 0) < size + 4 * constraints
    owns[...] = jnp.where(upper, high, low).astype(bf16)
    rows = out_ref.shape[0]
    block = rows // 4
    leaving = []
    for i in range(4):
        here = slice(i * block, (i + 1) * block)
        late = late_ref[here, :]
        combined = (part_ref[here, :] + dot(own_ref[here, :], owns[...])).astype(bf16).astype(f32)
        out_ref[here, :] = combined + (early_ref[here, :] + (dot(late, highs[...]) + dot(late, lows[...])))
        p = pl.ds(i * block, block)
        leaving.append(pltpu.make_async_copy(out_ref.at[p], out_any.at[p], sems.at[i]))
        leaving[-1].start()
    for leave in leaving:
        leave.wait()


def body(
    residual,
    scaling,
    local_inverse,
    coarse_basis,
    primal_map,
    slot_index,
    slot_length,
    coarse_sub,
    coarse_pivot,
):
    slabs, groups = lax.axis_size("wide"), lax.axis_size("narrow")
    residual, inverse = residual[0, 0], local_inverse[0, 0]
    basis = coarse_basis[0, 0]
    slots, capacity = slot_index.shape[2] - 1, slot_index.shape[3]
    index = slot_index.reshape(slots + 1, 1, capacity)
    length = slot_length[0]
    size = coarse_sub.shape[1]
    order = ceil_lanes(size)
    rows, columns = residual.shape
    constraints = basis.shape[0]
    own_columns = columns // groups
    quarter = own_columns // 4
    width = ceil_lanes(size + 5 * constraints)
    scale = scaling[0, 0].reshape(rows // LANES, LANES)
    lane_scale = scaling[0]
    struct = jax.ShapeDtypeStruct

    def by_lanes(count, block):
        return pl.BlockSpec((count, block), lambda i: (0, i))

    any_space = pl.BlockSpec(memory_space=pl.ANY)
    vmem = pl.BlockSpec(memory_space=pltpu.VMEM)
    n = lax.axis_index("narrow")
    factors = [jnp.where((n & 1) == 0, coarse_sub, coarse_pivot)]
    held, offsets = factors[0], [0]
    masks = [1 << i for i in reversed(range(slabs.bit_length() - 1))]
    masks[-2:] = masks[:-3:-1]
    for mask in masks:
        factors.append(swap(held, "wide", mask))
        offsets = offsets + [o ^ mask for o in offsets]
        if len(offsets) < slabs:
            held = join(factors)

    mine, other = [held, factors[-1]], []
    for piece in mine:
        other.append(swap(piece, "narrow", 1))

    sent, part, *outgoing = call(
        functools.partial(local_kernel, slabs, groups),
        [struct((slabs * groups, quarter, LANES), f32), struct((rows, columns), f32)]
        + [struct((capacity + GROUP, columns), bf16)] * slots,
        [any_space] * 7,
        (inverse, residual, scale, lane_scale, basis, index, primal_map[0]),
        out_specs=[any_space] * (2 + slots),
        scratch=[pltpu.VMEM((capacity + GROUP, columns), bf16)] * slots
        + [
            pltpu.VMEM((slabs * groups, quarter, LANES), f32),
            pltpu.VMEM(primal_map[0].shape, jnp.int32),
            pltpu.VMEM(lane_scale.shape, f32),
            pltpu.VMEM(basis.shape, bf16),
            pltpu.VMEM(index.shape, jnp.int32),
            pltpu.VMEM((rows, rows), bf16),
            pltpu.VMEM((rows, columns), bf16),
            pltpu.VMEM(scale.shape, f32),
            pltpu.VMEM((rows, columns), bf16),
            pltpu.VMEM((rows, columns), bf16),
            pltpu.VMEM((rows, columns), f32),
            pltpu.VMEM((constraints, rows), f32),
            pltpu.VMEM((slots, capacity, columns), f32),
            pltpu.SemaphoreType.DMA((8,)),
            pltpu.SemaphoreType.DMA((3 + slots,)),
        ],
        flops=2 * rows * columns * (rows + slots * capacity),
        limit=57,
    )
    got = lax.all_to_all(sent, ("wide", "narrow"), split_axis=0, concat_axis=0, tiled=True)
    arrived = []
    for k in range(slots):
        if k < groups - 1:
            arrived.append(swap(outgoing[k], "narrow", k + 1))
        elif k == groups - 1:
            arrived.append(swap(outgoing[k], "wide", 1))
        else:
            arrived.append(swap_odd(outgoing[k], "wide"))

    right, maps = call(
        functools.partial(unpack_kernel, slabs, groups, constraints),
        [struct((slabs, own_columns, order), f32), struct((slabs * groups, LANES), f32)],
        [None],
        (got,),
        flops=2 * slabs * 3 * own_columns * LANES * order,
    )
    shares = call(
        functools.partial(solve_kernel, slabs, groups, constraints, offsets),
        [struct((own_columns, width), f32)] * groups,
        [None] * (2 + len(mine) + len(other)),
        (right, maps, *mine, *other),
        scratch=[
            pltpu.VMEM((2, slabs, order, order), f32),
            pltpu.VMEM((slabs, order, 2 * order), bf16),
            pltpu.VMEM((slabs, order, 2 * order), bf16),
            pltpu.VMEM((slabs, order, 2 * order), bf16),
            pltpu.VMEM((slabs, own_columns, order), f32),
        ],
        flops=2 * 3 * slabs * 2 * own_columns * order * 2 * order,
        limit=24 if slabs <= 8 else 62,
    )
    pieces = [shares[0]] + [swap(shares[k], "narrow", k) for k in range(1, groups)]

    block = min(rows, 1024)
    early, late, own = call(
        functools.partial(scatter_kernel, groups, size),
        [struct((rows, columns), f32), struct((rows, width), bf16), struct((rows, width), bf16)],
        [None, None, None, by_lanes(1, block), by_lanes(constraints, block)] + [None] * slots,
        (length, index, maps, lane_scale, basis, *arrived),
        grid=(rows // block,),
        out_specs=[vmem] * 3,
        scratch=[
            pltpu.VMEM((slots * capacity, columns + width), bf16),
            pltpu.VMEM((1, slots * capacity), jnp.int32),
        ],
        flops=2 * rows * slots * capacity * (columns + width),
    )
    result = call(
        functools.partial(final_kernel, groups, size, constraints),
        struct((rows, columns), f32),
        [vmem] * 4 + [None] * groups,
        (part, early, late, own, *pieces),
        out_specs=any_space,
        scratch=[
            pltpu.VMEM((rows, columns), f32),
            pltpu.VMEM((columns, width), f32),
            pltpu.VMEM((width, columns), bf16),
            pltpu.VMEM((width, columns), bf16),
            pltpu.VMEM((width, columns), bf16),
            pltpu.SemaphoreType.DMA((4,)),
        ],
        flops=2 * rows * columns * 3 * width,
    )
    return result[None, None]


def solution(mesh):
    in_specs = (
        P("wide", "narrow", None, None),
        P("wide", "narrow", None),
        P("wide", "narrow", None, None),
        P("wide", "narrow", None, None),
        P("wide", "narrow", None),
        P("wide", "narrow", None, None),
        P("wide", "narrow", None),
        P("wide", None, None),
        P("wide", None, None),
    )
    out_specs = P("wide", "narrow", None, None)

    return jax.shard_map(body, mesh=mesh, in_specs=in_specs, out_specs=out_specs, check_vma=False)
```

```python
import functools

import jax
import jax.numpy as jnp
from jax import lax
from jax.experimental import pallas as pl
from jax.experimental.pallas import tpu as pltpu
from jax.sharding import PartitionSpec as P


f32 = jnp.float32
bf16 = jnp.bfloat16
LANES = 128
GROUP = 32


def swap(block, axis, mask):
    count = lax.axis_size(axis)
    return lax.ppermute(block, axis, [(i, i ^ mask) for i in range(count)])


def swap_odd(block, axis):
    count = lax.axis_size(axis)
    pairs = [(i, i + 1) for i in range(1, count - 1, 2)]
    return lax.ppermute(block, axis, pairs + [(b, a) for a, b in pairs])


def ceil_lanes(size):
    return -(-size // LANES) * LANES


def iota(shape, axis):
    return lax.broadcasted_iota(jnp.int32, shape, axis)


def dot(left, right):
    return jnp.dot(left, right, preferred_element_type=f32)


def split_two(value):
    high = value.astype(bf16)
    return high, (value - high.astype(f32)).astype(bf16)


def split_three(value):
    high = value.astype(bf16)
    rest = value - high.astype(f32)
    middle = rest.astype(bf16)
    return high, middle, (rest - middle.astype(f32)).astype(bf16)


def turned_scale(scale_ref):
    scale = scale_ref[...]
    return jnp.concatenate(
        [scale, jnp.zeros((LANES - scale.shape[0], LANES), f32)], axis=0
    ).T


def call(kernel, outs, in_specs, args, grid=(1,), out_specs=None, scratch=(), flops=0, limit=24):
    many = isinstance(outs, (list, tuple))
    resident = pl.BlockSpec(memory_space=pltpu.VMEM)
    if out_specs is None:
        out_specs = [resident] * len(outs) if many else resident
    in_specs = [resident if s is None else s for s in in_specs]
    sizes = [a.size * a.dtype.itemsize for a in list(args) + (list(outs) if many else [outs])]
    return pl.pallas_call(
        kernel,
        out_shape=outs,
        grid=grid,
        in_specs=in_specs,
        out_specs=out_specs,
        scratch_shapes=list(scratch),
        compiler_params=pltpu.CompilerParams(vmem_limit_bytes=limit << 20),
        cost_estimate=pl.CostEstimate(flops=flops, bytes_accessed=sum(sizes), transcendentals=0),
    )(*args)


def join_kernel(*refs):
    start = 0
    for ref in refs[:-1]:
        refs[-1][start : start + ref.shape[0]] = ref[...]
        start += ref.shape[0]


def join(parts):
    total = sum(p.shape[0] for p in parts)
    out = jax.ShapeDtypeStruct((total,) + parts[0].shape[1:], parts[0].dtype)
    return call(join_kernel, out, [None] * len(parts), parts)


def copies(sources, targets, sems):
    moves = [pltpu.make_async_copy(a, b, sems.at[i]) for i, (a, b) in enumerate(zip(sources, targets))]
    for move in moves:
        move.start()
    return moves


def weigh(scale_turned, res_ref, start, count):
    for j in range(count // LANES):
        row = start + j * LANES
        factor = scale_turned[:, row // LANES : row // LANES + 1]
        yield (factor * res_ref[row : row + LANES, :].astype(f32)).astype(bf16)


def pack_pieces(slabs, groups, primal, map_ref, sent_ref):
    constraints, columns = primal.shape
    turned = jnp.concatenate([primal, jnp.zeros((LANES - constraints, columns), f32)], axis=0).T
    quarter = sent_ref.shape[1]
    spare = GROUP - constraints
    code = map_ref[...].astype(f32)
    code = jnp.concatenate([code, jnp.zeros((1, LANES - constraints), f32)], axis=1)
    lanes = iota((1, LANES), 1)
    tail = jnp.zeros((1, LANES), f32)
    for q in range(-(-constraints // spare)):
        start = GROUP * q + constraints
        inside = (lanes >= start) & (lanes < start + min(spare, constraints - spare * q))
        tail = jnp.where(inside, pltpu.roll(code, start - spare * q, 1), tail)
    tail = jnp.where(iota((quarter, LANES), 0) == 0, tail, 0.0)
    for m in range(groups):
        piece = tail
        for g in range(4):
            start = (m * 4 + g) * quarter
            part = turned[start : start + quarter, :]
            piece = piece + (pltpu.roll(part, GROUP * g, 1) if g else part)
        for v in range(slabs):
            sent_ref[v * groups + m] = piece


def place_of():
    return lax.axis_index("wide"), lax.axis_index("narrow")


def slot_rows(groups):
    w, n = place_of()
    parity = w & 1
    return [n ^ k for k in range(1, groups)] + [groups + 1 - parity, groups + parity]


def local_kernel(slabs, groups, inverse_any, res_any, scale_any, lane_scale_any, basis_any, index_any, map_any, sent_any, part_any, *rest):
    slots = groups + 1
    outs_any, outs = rest[:slots], rest[slots : 2 * slots]
    sent_ref, map_ref, lane_scale_ref, basis_ref, index_ref, inverse_ref, res_ref, scale_ref, weighted_ref, narrow_ref, part_ref, scaled_ref, first_ref, sems, out_sems = rest[2 * slots :]
    rows = inverse_ref.shape[0]
    half = rows // 2
    halves = [pl.ds(i * half, half) for i in range(2)]
    sources = [scale_any, res_any, basis_any, map_any, lane_scale_any, index_any]
    targets = [scale_ref, res_ref, basis_ref, map_ref, lane_scale_ref, index_ref]
    sources += [inverse_any.at[p] for p in halves]
    targets += [inverse_ref.at[p] for p in halves]
    moves = copies(sources, targets, sems)
    for move in moves[:6]:
        move.wait()
    turned = turned_scale(scale_ref)
    for j, value in enumerate(weigh(turned, res_ref, 0, rows)):
        weighted_ref[j * LANES : (j + 1) * LANES, :] = value
    pack_pieces(slabs, groups, dot(basis_ref[...], weighted_ref[...]), map_ref, sent_ref)
    leaving = [pltpu.make_async_copy(sent_ref, sent_any, out_sems.at[2 + slots])]
    leaving[0].start()
    capacity = index_ref.shape[2]
    constraints = basis_ref.shape[0]
    picks = [index_ref[r] for r in slot_rows(groups)]
    scaled_ref[...] = lane_scale_ref[...] * basis_ref[...].astype(f32)
    for k in range(slots):
        parts = []
        for c in range(capacity // LANES):
            spot = jnp.broadcast_to(picks[k][:, c * LANES : (c + 1) * LANES], (constraints, LANES))
            inner, outer = spot & (LANES - 1), spot // LANES
            value = jnp.zeros((constraints, LANES), f32)
            for j in range(rows // LANES):
                found = jnp.take_along_axis(scaled_ref[:, j * LANES : (j + 1) * LANES], inner, axis=1)
                value = jnp.where(outer == j, found, value)
            parts.append(value)
        fill = jnp.zeros((GROUP - constraints, capacity), f32)
        outs[k][capacity:, :] = jnp.concatenate([jnp.concatenate(parts, axis=1), fill], axis=0).astype(bf16)
    spare_rows = [jnp.zeros((LANES - slots, capacity), jnp.int32)]
    columns_of = jnp.concatenate(picks + spare_rows, axis=0).astype(f32).T
    lanes = iota((capacity, LANES), 1).astype(f32)
    for i, p in enumerate(halves):
        moves[6 + i].wait()
        block = min(half, 256)
        for start in range(i * half, (i + 1) * half, block):
            part = dot(inverse_ref[start : start + block, :], weighted_ref[...])
            for j in range(block // LANES):
                row = start + j * LANES
                column = row // LANES
                scaled = turned[:, column : column + 1] * part[j * LANES : (j + 1) * LANES, :]
                part_ref[row : row + LANES, :] = scaled
                narrow_ref[row : row + LANES, :] = scaled.astype(bf16)
        leave = pltpu.make_async_copy(part_ref.at[p], part_any.at[p], out_sems.at[i])
        leave.start()
        leaving.append(leave)
        for k in range(slots):
            spot = jnp.broadcast_to(columns_of[:, k : k + 1], (capacity, LANES))
            hots = [
                (spot == lanes + float(j * LANES)).astype(f32).astype(bf16)
                for j in range(i * half // LANES, (i + 1) * half // LANES)
            ]
            found = dot(jnp.concatenate(hots, axis=1), narrow_ref[i * half : (i + 1) * half, :])
            if i == 0:
                first_ref[k] = found
                continue
            outs[k][:capacity, :] = (first_ref[k] + found).astype(bf16)
            leave = pltpu.make_async_copy(outs[k], outs_any[k], out_sems.at[2 + k])
            leave.start()
            leaving.append(leave)
    for leave in leaving:
        leave.wait()


def unpack_kernel(slabs, groups, constraints, got_ref, right_ref, maps_ref):
    pieces, quarter, _ = got_ref.shape
    spare = GROUP - constraints
    heads = jnp.concatenate([got_ref[i, 0:1, :] for i in range(pieces)], axis=0)
    lanes = iota((pieces, LANES), 1)
    maps = jnp.full((pieces, LANES), -1.0, f32)
    for q in range(-(-constraints // spare)):
        shift = (spare * q - GROUP * q - constraints) % LANES
        moved = pltpu.roll(heads, shift, 1) if shift else heads
        inside = (lanes >= spare * q) & (lanes < min(spare * (q + 1), constraints))
        maps = jnp.where(inside, moved, maps)
    maps_ref[...] = maps
    order = right_ref.shape[2]
    halves = groups * GROUP // LANES
    lanes = iota((quarter, LANES), 1) // GROUP
    wide = iota((1, LANES), 1) // GROUP

    def one(v, carry):
        value, codes = [], []
        for h in range(halves):
            rows = []
            for g in range(4):
                row = None
                for j in range(4):
                    part = got_ref[v * groups + 4 * h + j]
                    shift = (GROUP * (j - g)) % LANES
                    part = pltpu.roll(part, shift, 1) if shift else part
                    row = part if row is None else jnp.where(lanes == j, part, row)
                rows.append(row)
            value.append(jnp.concatenate(rows, axis=0))
            code = None
            for j in range(4):
                part = maps_ref[pl.ds(v * groups + 4 * h + j, 1), :]
                part = pltpu.roll(part, GROUP * j, 1) if j else part
                code = part if code is None else jnp.where(wide == j, part, code)
            codes.append(code)
        value = jnp.concatenate(value, axis=1) if halves > 1 else value[0]
        code = jnp.concatenate(codes, axis=1) if halves > 1 else codes[0]
        hot = (iota((order, halves * LANES), 0).astype(f32) == code).astype(f32).astype(bf16)
        stacked = jnp.concatenate(split_three(value), axis=0)
        total = lax.dot_general(stacked, hot, (((1,), (1,)), ((), ())), preferred_element_type=f32)
        c = value.shape[0]
        right_ref[v] = total[:c] + total[c : 2 * c] + total[2 * c :]
        return carry

    lax.fori_loop(0, slabs, one, 0, unroll=slabs <= 8)


def solve_kernel(slabs, groups, constraints, offsets, right_ref, maps_ref, *rest):
    mine, other, shares = rest[:2], rest[2:4], rest[4 : 4 + groups]
    raw, forward, backward, pivots, solved = rest[4 + groups :]
    w, n = place_of()
    core = n & 1
    size = mine[0].shape[2]
    order = raw.shape[2]
    if size != order:
        raw[...] = jnp.zeros_like(raw)
    start = 0
    for a, b in zip(mine, other):
        for i in range(a.shape[0]):
            slab = w ^ offsets[start + i]
            raw[core, slab, :size, :size] = a[i]
            raw[1 - core, slab, :size, :size] = b[i]
        start += a.shape[0]
    c = right_ref.shape[1]
    few = slabs <= 8

    def prepare(v, carry):
        sub = raw[0, v]
        for ref, value in ((forward, sub.T), (backward, sub), (pivots, raw[1, v])):
            high, low = split_two(value)
            ref[v, :, :order] = high
            ref[v, :, order:] = low
        return carry

    def times(value, factor):
        total = dot(jnp.concatenate(split_two(value), axis=0), factor)
        return total[:c, :order] + (total[:c, order:] + total[c:, :order])

    def down(v, value):
        value = right_ref[v] - times(value, forward[v])
        solved[v] = value
        return value

    def pivot(v, carry):
        solved[v] = times(solved[v], pivots[v])
        return carry

    def up(i, value):
        v = slabs - 2 - i
        value = solved[v] - times(value, backward[v + 1])
        solved[v] = value
        return value

    lax.fori_loop(0, slabs, prepare, 0, unroll=few)
    solved[0] = right_ref[0]
    lax.fori_loop(1, slabs, down, right_ref[0], unroll=few)
    lax.fori_loop(0, slabs, pivot, 0, unroll=few)
    lax.fori_loop(0, slabs - 1, up, solved[slabs - 1], unroll=few)

    parity = w & 1
    sides = [w, w ^ 1, jnp.clip(w - 1 + 2 * parity, 0, slabs - 1)]
    value = jnp.concatenate([solved[s] for s in sides], axis=1)
    stacked = jnp.concatenate(split_two(value), axis=0)
    width = shares[0].shape[1]
    lanes = iota((1, width), 1)
    rows = iota((order, width), 0).astype(f32)
    starts = [
        [size + (2 + i) * constraints for i in range(3)],
        [size],
        [size + constraints],
    ]
    for k in range(groups):
        hots = []
        for s, (side, places) in enumerate(zip(sides, starts)):
            code = maps_ref[pl.ds(side * groups + (n ^ k), 1), :]
            code = jnp.concatenate([code, jnp.full((1, width - LANES), -1.0, f32)], axis=1)
            full = jnp.where(lanes < size, lanes.astype(f32), -1.0) if s == 0 else jnp.full((1, width), -1.0, f32)
            for place in places:
                inside = (lanes >= place) & (lanes < place + constraints)
                full = jnp.where(inside, pltpu.roll(code, place, 1), full)
            hots.append((rows == full).astype(f32).astype(bf16))
        total = dot(stacked, jnp.concatenate(hots, axis=0))
        shares[k][...] = total[:c] + total[c:]


def scatter_kernel(groups, size, length_ref, index_ref, maps_ref, lane_scale_ref, basis_ref, *rest):
    slots = groups + 1
    arrived = rest[:slots]
    early_ref, late_ref, own_ref, joined, targets = rest[slots:]
    step = pl.program_id(0)
    columns, width = early_ref.shape[1], late_ref.shape[1]
    block = early_ref.shape[0] // pl.num_programs(0)
    here_rows = pl.ds(pl.multiple_of(step * block, block), block)
    constraints = basis_ref.shape[0]
    capacity = index_ref.shape[2]
    w, n = place_of()

    @pl.when(step == 0)
    def _():
        for k, r in enumerate(slot_rows(groups)):
            spot = index_ref[r]
            count = jnp.where(iota(length_ref.shape, 1) == r, length_ref[...], 0)
            live = iota((1, capacity), 1) < jnp.sum(count, axis=1, keepdims=True)
            targets[:, k * capacity : (k + 1) * capacity] = jnp.where(live, spot, -1)
            here = slice(k * capacity, (k + 1) * capacity)
            joined[here, :columns] = arrived[k][:capacity, :]
            lanes = iota((1, LANES), 1)
            if k < groups - 1:
                code = maps_ref[pl.ds(w * groups + (n ^ (k + 1)), 1), :]
            else:
                start = size + (k - groups + 1) * constraints
                code = jnp.where(lanes < constraints, lanes + start, -1).astype(f32)
            hot = (iota((width, LANES), 0).astype(f32) == code).astype(f32).astype(bf16)
            spread = dot(hot[:, :GROUP], arrived[k][capacity:, :])
            joined[here, columns:] = spread.T.astype(bf16)

    rows = iota((block, capacity), 0) + step * block
    hots = []
    for k in range(slots):
        target = targets[:, k * capacity : (k + 1) * capacity]
        hots.append((rows == target).astype(f32).astype(bf16))
    total = dot(jnp.concatenate(hots, axis=1), joined[...])
    early_ref[here_rows, :] = total[:, :columns]
    late_ref[here_rows, :] = total[:, columns:].astype(bf16)
    scaled = lane_scale_ref[...] * basis_ref[...].astype(f32)
    high = scaled.astype(bf16).astype(f32)
    start = size + 2 * constraints
    stop = start + 3 * constraints
    stack = jnp.concatenate(
        [jnp.zeros((start, block), f32), high, scaled - high, high, jnp.zeros((width - stop, block), f32)],
        axis=0,
    )
    own_ref[here_rows, :] = stack.T.astype(bf16)


def final_kernel(groups, size, constraints, part_ref, early_ref, late_ref, own_ref, *rest):
    pieces = rest[:groups]
    out_any, out_ref, values, highs, lows, owns, sems = rest[groups:]
    _, n = place_of()
    c = pieces[0].shape[0]
    for k in range(groups):
        values[pl.ds(pl.multiple_of((n ^ k) * c, c), c), :] = pieces[k][...]
    value = values[...].T
    high = value.astype(bf16).astype(f32)
    low = value - high
    highs[...] = high.astype(bf16)
    lows[...] = low.astype(bf16)
    upper = iota(value.shape, 0) < size + 4 * constraints
    owns[...] = jnp.where(upper, high, low).astype(bf16)
    rows = out_ref.shape[0]
    block = rows // 4
    leaving = []
    for i in range(4):
        here = slice(i * block, (i + 1) * block)
        late = late_ref[here, :]
        combined = (part_ref[here, :] + dot(own_ref[here, :], owns[...])).astype(bf16).astype(f32)
        out_ref[here, :] = combined + (early_ref[here, :] + (dot(late, highs[...]) + dot(late, lows[...])))
        p = pl.ds(i * block, block)
        leaving.append(pltpu.make_async_copy(out_ref.at[p], out_any.at[p], sems.at[i]))
        leaving[-1].start()
    for leave in leaving:
        leave.wait()


def body(
    residual,
    scaling,
    local_inverse,
    coarse_basis,
    primal_map,
    slot_index,
    slot_length,
    coarse_sub,
    coarse_pivot,
):
    slabs, groups = lax.axis_size("wide"), lax.axis_size("narrow")
    residual, inverse = residual[0, 0], local_inverse[0, 0]
    basis = coarse_basis[0, 0]
    slots, capacity = slot_index.shape[2] - 1, slot_index.shape[3]
    index = slot_index.reshape(slots + 1, 1, capacity)
    length = slot_length[0]
    size = coarse_sub.shape[1]
    order = ceil_lanes(size)
    rows, columns = residual.shape
    constraints = basis.shape[0]
    own_columns = columns // groups
    quarter = own_columns // 4
    width = ceil_lanes(size + 5 * constraints)
    scale = scaling[0, 0].reshape(rows // LANES, LANES)
    lane_scale = scaling[0]
    struct = jax.ShapeDtypeStruct

    def by_lanes(count, block):
        return pl.BlockSpec((count, block), lambda i: (0, i))

    any_space = pl.BlockSpec(memory_space=pl.ANY)
    vmem = pl.BlockSpec(memory_space=pltpu.VMEM)
    n = lax.axis_index("narrow")
    factors = [jnp.where((n & 1) == 0, coarse_sub, coarse_pivot)]
    held, offsets = factors[0], [0]
    masks = [1 << i for i in reversed(range(slabs.bit_length() - 1))]
    masks[-2:] = masks[:-3:-1]
    for mask in masks:
        factors.append(swap(held, "wide", mask))
        offsets = offsets + [o ^ mask for o in offsets]
        if len(offsets) < slabs:
            held = join(factors)

    mine, other = [held, factors[-1]], []
    for piece in mine:
        other.append(swap(piece, "narrow", 1))

    sent, part, *outgoing = call(
        functools.partial(local_kernel, slabs, groups),
        [struct((slabs * groups, quarter, LANES), f32), struct((rows, columns), f32)]
        + [struct((capacity + GROUP, columns), bf16)] * slots,
        [any_space] * 7,
        (inverse, residual, scale, lane_scale, basis, index, primal_map[0]),
        out_specs=[any_space] * (2 + slots),
        scratch=[pltpu.VMEM((capacity + GROUP, columns), bf16)] * slots
        + [
            pltpu.VMEM((slabs * groups, quarter, LANES), f32),
            pltpu.VMEM(primal_map[0].shape, jnp.int32),
            pltpu.VMEM(lane_scale.shape, f32),
            pltpu.VMEM(basis.shape, bf16),
            pltpu.VMEM(index.shape, jnp.int32),
            pltpu.VMEM((rows, rows), bf16),
            pltpu.VMEM((rows, columns), bf16),
            pltpu.VMEM(scale.shape, f32),
            pltpu.VMEM((rows, columns), bf16),
            pltpu.VMEM((rows, columns), bf16),
            pltpu.VMEM((rows, columns), f32),
            pltpu.VMEM((constraints, rows), f32),
            pltpu.VMEM((slots, capacity, columns), f32),
            pltpu.SemaphoreType.DMA((8,)),
            pltpu.SemaphoreType.DMA((3 + slots,)),
        ],
        flops=2 * rows * columns * (rows + slots * capacity),
        limit=57,
    )
    got = lax.all_to_all(sent, ("wide", "narrow"), split_axis=0, concat_axis=0, tiled=True)
    arrived = []
    for k in range(slots):
        if k < groups - 1:
            arrived.append(swap(outgoing[k], "narrow", k + 1))
        elif k == groups - 1:
            arrived.append(swap(outgoing[k], "wide", 1))
        else:
            arrived.append(swap_odd(outgoing[k], "wide"))

    right, maps = call(
        functools.partial(unpack_kernel, slabs, groups, constraints),
        [struct((slabs, own_columns, order), f32), struct((slabs * groups, LANES), f32)],
        [None],
        (got,),
        flops=2 * slabs * 3 * own_columns * LANES * order,
    )
    shares = call(
        functools.partial(solve_kernel, slabs, groups, constraints, offsets),
        [struct((own_columns, width), f32)] * groups,
        [None] * (2 + len(mine) + len(other)),
        (right, maps, *mine, *other),
        scratch=[
            pltpu.VMEM((2, slabs, order, order), f32),
            pltpu.VMEM((slabs, order, 2 * order), bf16),
            pltpu.VMEM((slabs, order, 2 * order), bf16),
            pltpu.VMEM((slabs, order, 2 * order), bf16),
            pltpu.VMEM((slabs, own_columns, order), f32),
        ],
        flops=2 * 3 * slabs * 2 * own_columns * order * 2 * order,
        limit=24 if slabs <= 8 else 62,
    )
    pieces = [shares[0]]
    for k in range(1, groups):
        pieces.append(swap(shares[k], "narrow", k))

    block = min(rows, 2048)
    early, late, own = call(
        functools.partial(scatter_kernel, groups, size),
        [struct((rows, columns), f32), struct((rows, width), bf16), struct((rows, width), bf16)],
        [None, None, None, by_lanes(1, block), by_lanes(constraints, block)] + [None] * slots,
        (length, index, maps, lane_scale, basis, *arrived),
        grid=(rows // block,),
        out_specs=[vmem] * 3,
        scratch=[
            pltpu.VMEM((slots * capacity, columns + width), bf16),
            pltpu.VMEM((1, slots * capacity), jnp.int32),
        ],
        flops=2 * rows * slots * capacity * (columns + width),
    )
    result = call(
        functools.partial(final_kernel, groups, size, constraints),
        struct((rows, columns), f32),
        [vmem] * 4 + [None] * groups,
        (part, early, late, own, *pieces),
        out_specs=any_space,
        scratch=[
            pltpu.VMEM((rows, columns), f32),
            pltpu.VMEM((columns, width), f32),
            pltpu.VMEM((width, columns), bf16),
            pltpu.VMEM((width, columns), bf16),
            pltpu.VMEM((width, columns), bf16),
            pltpu.SemaphoreType.DMA((4,)),
        ],
        flops=2 * rows * columns * 3 * width,
    )
    return result[None, None]


def solution(mesh):
    in_specs = (
        P("wide", "narrow", None, None),
        P("wide", "narrow", None),
        P("wide", "narrow", None, None),
        P("wide", "narrow", None, None),
        P("wide", "narrow", None),
        P("wide", "narrow", None, None),
        P("wide", "narrow", None),
        P("wide", None, None),
        P("wide", None, None),
    )
    out_specs = P("wide", "narrow", None, None)

    return jax.shard_map(body, mesh=mesh, in_specs=in_specs, out_specs=out_specs, check_vma=False)
```
